256 devices in a mesh: ctx: 32 (over z, x_hi, core), kv: 8 (over y, x_lo).
Axes of the slice: x: 4 (x_hi: 2, x_lo: 2; x = x_hi * 2 + x_lo), y: 4, z: 8, core: 2. Of those that a mesh axis runs over, the one named last changes fastest.
Arguments:
- queries: bfloat16 [6144, 5120], P('ctx', 'kv'), may hold values from -16 to 16
- keys: bfloat16 [6144, 1024], P('ctx', 'kv'), may hold values from -8 to 8
- values: bfloat16 [6144, 1024], P('ctx', 'kv'), may hold values from -6 to 6
- w_out: bfloat16 [5120, 5120], P('kv', 'ctx'), may hold values from -0.078125 to 0.078125
- grad_y: bfloat16 [6144, 5120], P('ctx', 'kv'), may hold values from -6 to 6
- resp_blocks: int32 [4], replicated, may hold values from 1 to 12, 24 in all
Outputs:
- y_out: bfloat16 [6144, 5120], P('ctx', 'kv')
- grad_q: bfloat16 [6144, 5120], P('ctx', 'kv')
- grad_k: bfloat16 [6144, 1024], P('ctx', 'kv')
- grad_v: bfloat16 [6144, 1024], P('ctx', 'kv')
The draws below stay inside these ranges and needn't reach their ends.
Inputs may be any that keep to these rules, and one draw needn't show every extreme that they name: resp_blocks sums to 24; the longest response has exactly 12 blocks.
All inputs are finite; a program needn't handle non-finite values.
Results may differ from the reference program's by a relative error of at most 0.035.
Values may be sent and summed in bfloat16 or wider, within the bound.
No kernel may reach another device: no remote copies, remote signals or barrier semaphores. Data moves between devices by JAX's collectives and lax.ppermute only.
A program may use at most 64 MiB of HBM per device.

```python
import math
import jax
import jax.numpy as jnp
import numpy as np
from jax import lax

D = 5120
H = 40
KVH = 8
HD = 128
BLK = 128
NRESP = 4
TOK_DEV = 192
TOKENS = 6144
PROMPT = 3072
RESP_BLOCKS = 24
MOST_BLOCKS = 12
N_KV = 8


def paired_draw(key):
    key_vals = jnp.clip(jax.random.normal(jax.random.fold_in(key, 11), (TOKENS, KVH * HD), jnp.float32), -4.5, 4.5)
    query_vals = jnp.clip(jax.random.normal(jax.random.fold_in(key, 12), (TOKENS, H * HD), jnp.float32), -4.5, 4.5)
    return (query_vals, key_vals)


def draw_queries(key, part):
    return paired_draw(key)[0].astype(jnp.bfloat16)


def draw_keys(key, part):
    return paired_draw(key)[1].astype(jnp.bfloat16)


def level_of(rng, dims, shards, smallest, largest):
    level = 1.0
    for position, shards_of in shards:
        steps = jax.random.uniform(jax.random.fold_in(jax.random.fold_in(rng, 6), position), (shards_of,), jnp.float32, smallest / len(shards), largest / len(shards))
        level = level * jnp.repeat(jnp.exp(steps), dims[position] // shards_of).reshape((-1,) + (1,) * (len(dims) - 1 - position))
    return level


def length_profile(number_of, total, bound, skew):
    loads = [(1 << 20) // math.isqrt(rank ** skew) + 1 for rank in range(2, number_of + 1)]
    rest, holding = total - bound - (number_of - 1), [1] * (number_of - 1)
    while rest > 0:
        candidates = [i for i in range(number_of - 1) if holding[i] < bound]
        whole, budget = sum([loads[i] for i in candidates]), rest
        for i in candidates:
            more = min(bound - holding[i], max(1, budget * loads[i] // whole), rest)
            holding[i] = holding[i] + more
            rest = rest - more
    return np.array([bound] + holding)


def uneven_parts(stream_key, count, total, reach, skew):
    if count == 2:
        one = jax.random.randint(stream_key, (), max(1, total - reach), min(reach, total - 1) + 1)
        return jnp.stack([one, total - one])
    lengths = jnp.asarray(length_profile(count, total, reach, skew), jnp.int32)
    twos = (count - 1) // 2
    source_of, taker = lengths[1:1 + 2 * twos:2], lengths[2:2 + 2 * twos:2]
    slack = jnp.minimum(source_of - 1, reach - taker)
    passed = jax.random.randint(jax.random.fold_in(stream_key, 1), (twos,), 0, 1 << 20) % (slack + 1)
    lengths = lengths.at[1:1 + 2 * twos:2].set(source_of - passed).at[2:2 + 2 * twos:2].set(taker + passed)
    return lengths[jax.random.permutation(jax.random.fold_in(stream_key, 2), count)]


def normal_values(own_key, dims, spread, reach, cuts=(), kind=jnp.bfloat16):
    array = spread * jax.random.normal(own_key, dims, jnp.float32)
    if cuts:
        array = array * level_of(own_key, dims, cuts, -0.22, 0.18)
    return jnp.clip(array, -reach, reach).astype(kind)


def setup_inputs(seed: int = 0) -> dict:
    seeds = jax.random.split(jax.random.key(seed), 7)
    queries = draw_queries(jax.random.fold_in(seeds[6], 71), 0)
    keys = draw_keys(jax.random.fold_in(seeds[6], 71), 0)
    values = normal_values(seeds[2], (TOKENS, KVH * HD), 1.0, 6.0, ((0, 32), (1, 8)))
    w_out = normal_values(seeds[3], (H * HD, D), (H * HD) ** -0.5, 0.078125, ((0, 8), (1, 32)))
    grad_y = normal_values(seeds[4], (TOKENS, D), 1.0, 6.0, ((0, 32), (1, 8)))
    resp_blocks = uneven_parts(seeds[5], NRESP, RESP_BLOCKS, MOST_BLOCKS, 1).astype(jnp.int32)
    return dict(queries=queries, keys=keys, values=values, w_out=w_out, grad_y=grad_y, resp_blocks=resp_blocks)


NEG = -1e+30

def segment_ids(positions, resp_blocks, prompt_len):
    resp_ends = jnp.cumsum(resp_blocks).astype(jnp.int32) * BLK
    offsets = positions - prompt_len
    later = lax.optimization_barrier(jnp.sum((offsets[:, None] >= resp_ends[None, :NRESP - 1]).astype(jnp.int32), axis=1))
    return jnp.where(positions < prompt_len, 0, 1 + later).astype(jnp.int32)

def visible_pairs(query_pos, query_seg, key_pos, key_seg):
    causal = key_pos[None, :] <= query_pos[:, None]
    same = (key_seg[None, :] == 0) | (key_seg[None, :] == query_seg[:, None])
    return causal & same

def rounded(values_in):
    return lax.optimization_barrier(values_in.astype(jnp.bfloat16)).astype(jnp.float32)

def reference(queries, keys, values, w_out, grad_y, resp_blocks):
    group_size = H // KVH
    score_scale = 1.0 / math.sqrt(HD)
    qblock = TOK_DEV
    block_total = TOKENS // qblock
    positions = jnp.arange(TOKENS, dtype=jnp.int32)
    segments = segment_ids(positions, resp_blocks, PROMPT)
    grad_attn = jnp.dot(grad_y, w_out.T, preferred_element_type=jnp.float32).astype(jnp.bfloat16)
    q_heads = queries.reshape(TOKENS, KVH, group_size, HD).transpose(1, 0, 2, 3)
    d_heads = grad_attn.reshape(TOKENS, KVH, group_size, HD).transpose(1, 0, 2, 3)
    k_heads = keys.reshape(TOKENS, KVH, HD).transpose(1, 0, 2)
    v_heads = values.reshape(TOKENS, KVH, HD).transpose(1, 0, 2)

    def one_head(operands):
        q_one, k_one, v_one, d_one = operands
        k_full = k_one.astype(jnp.float32)
        v_full = v_one.astype(jnp.float32)

        def one_block(grads, block_index):
            first = (block_index * qblock).astype(jnp.int32)
            q_rows = lax.dynamic_slice_in_dim(q_one, first, qblock, 0).astype(jnp.float32)
            d_rows = lax.dynamic_slice_in_dim(d_one, first, qblock, 0).astype(jnp.float32)
            query_pos = first + jnp.arange(qblock, dtype=jnp.int32)
            query_seg = lax.dynamic_slice_in_dim(segments, first, qblock, 0)
            visible = visible_pairs(query_pos, query_seg, positions, segments)
            scores = jnp.einsum('tgd,sd->gts', q_rows, k_full) * score_scale
            masked = jnp.where(visible[None], scores, NEG)
            top = lax.optimization_barrier(jnp.max(masked, axis=-1))
            weights = jnp.where(visible[None], jnp.exp(masked - top[..., None]), 0.0)
            norm_sum = lax.optimization_barrier(jnp.sum(weights, axis=-1))
            log_sum = top + jnp.log(norm_sum)
            attn = jnp.einsum('gts,sd->tgd', rounded(weights), v_full) / norm_sum.T[..., None]
            attn_b = attn.astype(jnp.bfloat16)
            delta = lax.optimization_barrier(jnp.sum(rounded(attn) * d_rows, axis=-1)).T
            probs = jnp.where(visible[None], jnp.exp(masked - log_sum[..., None]), 0.0)
            value_grad = jnp.einsum('gts,tgd->sd', rounded(probs), d_rows)
            prob_grad = jnp.einsum('tgd,sd->gts', d_rows, v_full)
            score_grad = rounded(probs * (prob_grad - delta[..., None]))
            query_grad = jnp.einsum('gts,sd->tgd', score_grad, k_full) * score_scale
            key_grad = jnp.einsum('gts,tgd->sd', score_grad, q_rows) * score_scale
            return ((grads[0] + rounded(key_grad), grads[1] + rounded(value_grad)), (attn_b, query_grad.astype(jnp.bfloat16)))
        zeros = jnp.zeros((TOKENS, HD), jnp.float32)
        (key_sum, value_sum), (attn_blocks, query_blocks) = lax.scan(one_block, (zeros, zeros), jnp.arange(block_total, dtype=jnp.int32))
        return (attn_blocks.reshape(TOKENS, group_size, HD), query_blocks.reshape(TOKENS, group_size, HD), key_sum.astype(jnp.bfloat16), value_sum.astype(jnp.bfloat16))
    attn_all, grad_q, grad_k, grad_v = lax.map(one_head, (q_heads, k_heads, v_heads, d_heads))
    attn_rows = attn_all.transpose(1, 0, 2, 3).reshape(TOKENS, H * HD)
    group_rows = H * HD // N_KV
    y_total = jnp.zeros((TOKENS, D), jnp.float32)
    for group in range(N_KV):
        part_rows = attn_rows[:, group * group_rows:(group + 1) * group_rows]
        part_weight = w_out[group * group_rows:(group + 1) * group_rows]
        y_total = y_total + rounded(jnp.dot(part_rows, part_weight, preferred_element_type=jnp.float32))
    y_out = y_total.astype(jnp.bfloat16)
    grad_q = grad_q.transpose(1, 0, 2, 3).reshape(TOKENS, H * HD)
    grad_k = grad_k.transpose(1, 0, 2).reshape(TOKENS, KVH * HD)
    grad_v = grad_v.transpose(1, 0, 2).reshape(TOKENS, KVH * HD)
    return (y_out, grad_q, grad_k, grad_v)
```

```python
import math

import jax
import jax.numpy as jnp
from jax import lax
from jax.experimental import pallas as pl
from jax.experimental.pallas import tpu as pltpu
from jax.sharding import Mesh
from jax.sharding import PartitionSpec as P

GROUP = 5
HD = 128
BLK = 128
NRESP = 4
NZ = 8
TOK = 192
ROWS = 1024
TILE = 256
HALF = 2 * TOK
CHUNK = 4 * TOK
PROMPT = 4 * CHUNK
NEG = -1e30
SCALE = 1.0 / math.sqrt(HD)
SCALE2 = SCALE * math.log2(math.e)
CTX = ("z", "xh", "c")
KV = ("y", "xl")
F32 = jnp.float32
BF16 = jnp.bfloat16


def shift(x, axis, by, size):
    return lax.ppermute(x, axis, [(i, (i + by) % size) for i in range(size)])


def dot(a, b):
    return jnp.dot(a, b, preferred_element_type=F32)


def ring_gather(own):
    rows = own.shape[0] // 2
    up, down = own, own
    blocks = {0: own}
    for step in range(1, NZ // 2):
        up, down = shift(up, "z", 1, NZ), shift(down, "z", -1, NZ)
        blocks[NZ - step], blocks[step] = up, down
    far_up = shift(up[:rows], "z", 1, NZ)
    far_down = shift(down[rows:], "z", -1, NZ)
    blocks[NZ // 2] = jnp.concatenate([far_up, far_down], 0)
    return [blocks[k] for k in range(NZ)]


def add(a, b):
    return (a.astype(F32) + b.astype(F32)).astype(BF16)


def ring_reduce(parts):
    rows = parts[0].shape[0] // 2
    far = NZ // 2
    up = shift(parts[far][:rows], "z", 1, NZ)
    down = shift(parts[far][rows:], "z", -1, NZ)
    up = jnp.concatenate([add(parts[far - 1][:rows], up), parts[far - 1][rows:]], 0)
    down = jnp.concatenate([parts[far + 1][:rows], add(parts[far + 1][rows:], down)], 0)
    up, down = shift(up, "z", 1, NZ), shift(down, "z", -1, NZ)
    for step in range(far - 2, 0, -1):
        up, down = add(parts[step], up), add(parts[NZ - step], down)
        up, down = shift(up, "z", 1, NZ), shift(down, "z", -1, NZ)
    return parts[0].astype(F32) + (up.astype(F32) + down.astype(F32))


def head_rows(x_ref, rows_ref):
    for h in range(GROUP):
        rows_ref[h * TOK : (h + 1) * TOK, :] = x_ref[:, h * HD : (h + 1) * HD]
    rows_ref[GROUP * TOK :, :] = jnp.zeros((ROWS - GROUP * TOK, HD), rows_ref.dtype)


def flip(x):
    return x.astype(F32).T


def visible_tile(pos, qinfo_ref, tile, chunk):
    cols = slice(tile * TILE, (tile + 1) * TILE)
    query_pos = qinfo_ref[0:1, cols]
    first = jnp.where(chunk < PROMPT // CHUNK, 0, qinfo_ref[1:2, cols])
    return (pos <= query_pos) & (pos >= first)


def forward_kernel(
    flags_ref, chunk_ref, q_ref, mine_ref, other_ref, posr_ref, qinfo_ref,
    attn_ref, attn_t_ref, lse_ref, rows_ref, q_t_ref, top_ref, sum_ref, acc_ref,
):
    head_rows(q_ref, rows_ref)
    q_t_ref[...] = flip(rows_ref[...]).astype(BF16)
    top_ref[...] = jnp.full_like(top_ref, NEG)
    sum_ref[...] = jnp.zeros_like(sum_ref)
    acc_ref[...] = jnp.zeros_like(acc_ref)

    def step(k, masked):
        chunk = chunk_ref[k]
        at = pl.ds(pl.multiple_of(k * HALF, HALF), HALF)
        both = jnp.concatenate([mine_ref[at, :], other_ref[at, :]], 0)
        keys, values = both[:, :HD], both[:, HD:]
        values_t = flip(values).astype(BF16)
        pos = posr_ref[:, 0:1] + chunk * CHUNK
        for tile in range(ROWS // TILE):
            cols = slice(tile * TILE, (tile + 1) * TILE)
            scores = dot(keys, q_t_ref[:, cols]) * SCALE2
            if masked:
                scores = jnp.where(visible_tile(pos, qinfo_ref, tile, chunk), scores, NEG)
            old = top_ref[0:1, cols]
            top = jnp.maximum(old, jnp.max(scores, axis=0, keepdims=True))
            weights = jnp.exp2(scores - top)
            factor = jnp.exp2(old - top)
            top_ref[0:1, cols] = top
            sum_ref[0:1, cols] = sum_ref[0:1, cols] * factor + jnp.sum(weights, axis=0, keepdims=True)
            acc_ref[:, cols] = acc_ref[:, cols] * factor + dot(values_t, weights.astype(BF16))

    def body(k, carry):
        @pl.when(flags_ref[k] == 1)
        def _():
            step(k, False)

        @pl.when(flags_ref[k] == 2)
        def _():
            step(k, True)

        return carry

    lax.fori_loop(0, NZ, body, 0)
    lse_ref[...] = jnp.broadcast_to(top_ref[0:1, :] + jnp.log2(sum_ref[0:1, :]), lse_ref.shape)
    attn_t = acc_ref[...] / sum_ref[0:1, :]
    attn_t_ref[...] = attn_t.astype(BF16)
    attn = attn_t.T.astype(BF16)
    for h in range(GROUP):
        attn_ref[:, h * HD : (h + 1) * HD] = attn[h * TOK : (h + 1) * TOK, :]


def backward_kernel(
    flags_ref, chunk_ref, q_ref, g_ref, mine_ref, other_ref, posr_ref, qinfo_ref, attn_t_ref, lse_ref,
    dq_ref, dmine_ref, dother_ref, rows_ref, q_t_ref, g_rows_ref, g_t_ref, delta_ref, dq_t_ref, dk_ref, dv_ref,
):
    head_rows(q_ref, rows_ref)
    q_t_ref[...] = flip(rows_ref[...]).astype(BF16)
    head_rows(g_ref, g_rows_ref)
    g_t = flip(g_rows_ref[...])
    g_t_ref[...] = g_t.astype(BF16)
    delta_ref[0:1, :] = jnp.sum(g_t * attn_t_ref[...].astype(F32), axis=0, keepdims=True)
    dq_t_ref[...] = jnp.zeros_like(dq_t_ref)

    def step(k, masked):
        chunk = chunk_ref[k]
        at = pl.ds(pl.multiple_of(k * HALF, HALF), HALF)
        both = jnp.concatenate([mine_ref[at, :], other_ref[at, :]], 0)
        keys, values = both[:, :HD], both[:, HD:]
        keys_t = flip(keys).astype(BF16)
        pos = posr_ref[:, 0:1] + chunk * CHUNK
        for tile in range(ROWS // TILE):
            cols = slice(tile * TILE, (tile + 1) * TILE)
            scores = dot(keys, q_t_ref[:, cols]) * SCALE2
            if masked:
                scores = jnp.where(visible_tile(pos, qinfo_ref, tile, chunk), scores, NEG)
            probs = jnp.exp2(scores - lse_ref[0:1, cols])
            dv = dot(probs.astype(BF16), g_rows_ref[cols, :])
            grads = probs * (dot(values, g_t_ref[:, cols]) - delta_ref[0:1, cols])
            grads = grads.astype(BF16)
            dk = dot(grads, rows_ref[cols, :])
            dv_ref[...] = dv if tile == 0 else dv_ref[...] + dv
            dk_ref[...] = dk if tile == 0 else dk_ref[...] + dk
            dq_t_ref[:, cols] += dot(keys_t, grads)
        dk, dv = (dk_ref[...] * SCALE).astype(BF16), dv_ref[...].astype(BF16)
        dmine_ref[at, :HD] = dk[:HALF]
        dmine_ref[at, HD:] = dv[:HALF]
        dother_ref[at, :HD] = dk[HALF:]
        dother_ref[at, HD:] = dv[HALF:]

    def body(k, carry):
        @pl.when(flags_ref[k] == 0)
        def _():
            at = pl.ds(pl.multiple_of(k * HALF, HALF), HALF)
            dmine_ref[at, :] = jnp.zeros((HALF, 2 * HD), BF16)
            dother_ref[at, :] = jnp.zeros((HALF, 2 * HD), BF16)

        @pl.when(flags_ref[k] == 1)
        def _():
            step(k, False)

        @pl.when(flags_ref[k] == 2)
        def _():
            step(k, True)

        return carry

    lax.fori_loop(0, NZ, body, 0)
    dq = (dq_t_ref[...].T * SCALE).astype(BF16)
    for h in range(GROUP):
        dq_ref[:, h * HD : (h + 1) * HD] = dq[h * TOK : (h + 1) * TOK, :]


SMEM = pl.BlockSpec(memory_space=pltpu.SMEM)
VMEM = pl.BlockSpec(memory_space=pltpu.VMEM)
PARAMS = pltpu.CompilerParams(vmem_limit_bytes=48 << 20)


def forward(flags, chunks, q, mine, other, posr, qinfo):
    return pl.pallas_call(
        forward_kernel,
        out_shape=(
            jax.ShapeDtypeStruct((TOK, GROUP * HD), BF16),
            jax.ShapeDtypeStruct((HD, ROWS), BF16),
            jax.ShapeDtypeStruct((8, ROWS), F32),
        ),
        in_specs=[SMEM, SMEM] + [VMEM] * 5,
        out_specs=(VMEM,) * 3,
        scratch_shapes=[
            pltpu.VMEM((ROWS, HD), BF16),
            pltpu.VMEM((HD, ROWS), BF16),
            pltpu.VMEM((8, ROWS), F32),
            pltpu.VMEM((8, ROWS), F32),
            pltpu.VMEM((HD, ROWS), F32),
        ],
        compiler_params=PARAMS,
        cost_estimate=pl.CostEstimate(flops=4 * 960 * 4608 * 128, bytes_accessed=4 << 20, transcendentals=960 * 4608),
        name="forward",
    )(flags, chunks, q, mine, other, posr, qinfo)


def backward(flags, chunks, q, g, mine, other, posr, qinfo, attn_t, lse):
    return pl.pallas_call(
        backward_kernel,
        out_shape=(
            jax.ShapeDtypeStruct((TOK, GROUP * HD), BF16),
            jax.ShapeDtypeStruct((NZ * HALF, 2 * HD), BF16),
            jax.ShapeDtypeStruct((NZ * HALF, 2 * HD), BF16),
        ),
        in_specs=[SMEM, SMEM] + [VMEM] * 8,
        out_specs=(VMEM,) * 3,
        scratch_shapes=[
            pltpu.VMEM((ROWS, HD), BF16),
            pltpu.VMEM((HD, ROWS), BF16),
            pltpu.VMEM((ROWS, HD), BF16),
            pltpu.VMEM((HD, ROWS), BF16),
            pltpu.VMEM((8, ROWS), F32),
            pltpu.VMEM((HD, ROWS), F32),
            pltpu.VMEM((CHUNK, HD), F32),
            pltpu.VMEM((CHUNK, HD), F32),
        ],
        compiler_params=PARAMS,
        cost_estimate=pl.CostEstimate(flops=10 * 960 * 4608 * 128, bytes_accessed=8 << 20, transcendentals=960 * 4608),
        name="backward",
    )(flags, chunks, q, g, mine, other, posr, qinfo, attn_t, lse)


def tables(resp_blocks):
    z, xh, c = lax.axis_index("z"), lax.axis_index("xh"), lax.axis_index("c")
    row = jnp.arange(CHUNK, dtype=jnp.int32)
    core = jnp.where(row < HALF, c, 1 - c)
    posr = core * TOK + (row % HALF) // TOK * HALF + row % TOK
    posr = jnp.broadcast_to(posr[:, None], (CHUNK, 128))
    first = z * CHUNK + xh * HALF + c * TOK
    query_pos = first + jnp.arange(ROWS, dtype=jnp.int32) % TOK
    end, start = jnp.int32(PROMPT), jnp.full((ROWS,), PROMPT, jnp.int32)
    for r in range(NRESP - 1):
        end = end + resp_blocks[r] * BLK
        start = jnp.where(query_pos >= end, end, start)
    qinfo = jnp.concatenate(
        [query_pos[None], start[None], jnp.zeros((6, ROWS), jnp.int32)], 0
    )
    chunks = (z + jnp.arange(NZ, dtype=jnp.int32)) % NZ
    earlier = (chunks < PROMPT // CHUNK) | ((chunks + 1) * CHUNK > jnp.min(start))
    kind = jnp.where(chunks < PROMPT // CHUNK, 1, 2)
    flags = jnp.where(chunks == z, 2, jnp.where((chunks < z) & earlier, kind, 0))
    return flags, chunks, posr, qinfo


def local(queries, keys, values, w_out, grad_y, resp_blocks):
    xh = lax.axis_index("xh")
    flags, chunks, posr, qinfo = tables(resp_blocks)
    weight = lax.all_gather(w_out.T, CTX, axis=0, tiled=True)
    grad_full = lax.all_gather(grad_y, KV, axis=1, tiled=True)

    own = jnp.concatenate([keys, values], 1)
    partner = shift(own, "xh", 1, 2)
    own = jnp.where(xh == 0, jnp.concatenate([own, partner], 0), jnp.concatenate([partner, own], 0))
    mine = jnp.concatenate(ring_gather(own), 0)
    other = shift(mine, "c", 1, 2)

    attn, attn_t, lse = forward(flags, chunks, queries, mine, other, posr, qinfo)
    grad_attn = dot(grad_full, weight).astype(BF16)
    y_terms = lax.dot_general(attn, weight, (((1,), (1,)), ((), ())), preferred_element_type=F32).astype(BF16)
    y_out = lax.psum_scatter(y_terms, KV, scatter_dimension=1, tiled=True)
    grad_q, dmine, dother = backward(
        flags, chunks, queries, grad_attn, mine, other, posr, qinfo, attn_t, lse
    )
    terms = add(dmine, shift(dother, "c", 1, 2))
    total = ring_reduce([terms[k * HALF : (k + 1) * HALF] for k in range(NZ)])
    low, high = total[:TOK], total[TOK:]
    send = jnp.where(xh == 0, high, low).astype(BF16)
    total = jnp.where(xh == 0, low, high) + shift(send, "xh", 1, 2).astype(F32)
    total = total.astype(BF16)
    return y_out, grad_q, total[:, :HD], total[:, HD:]


def solution(mesh):
    fine = Mesh(mesh.devices.reshape(NZ, 2, 2, 4, 2), CTX + KV)
    both = P(CTX, KV)
    return jax.shard_map(
        local,
        mesh=fine,
        in_specs=(both, both, both, P(KV, CTX), both, P()),
        out_specs=(both,) * 4,
        check_vma=False,
    )
```

```python
import functools
import math

import jax
import jax.numpy as jnp
from jax import lax
from jax.experimental import pallas as pl
from jax.experimental.pallas import tpu as pltpu
from jax.sharding import Mesh
from jax.sharding import PartitionSpec as P

GROUP = 5
HD = 128
BLK = 128
NRESP = 4
NZ = 8
NKV = 8
TOK = 192
COLS = 160
ROWS = 1024
TILE = 256
HALF = 2 * TOK
CHUNK = 4 * TOK
PROMPT = 4 * CHUNK
PART = 2 * TOK + GROUP * COLS
WIDTH = GROUP * HD
NEG = -1e30
SCALE = 1.0 / math.sqrt(HD)
SCALE2 = SCALE * math.log2(math.e)
CTX = ("z", "xh", "c")
KV = ("y", "xl")
F32 = jnp.float32
BF16 = jnp.bfloat16


def shift(x, axis, by, size):
    return lax.ppermute(x, axis, [(i, (i + by) % size) for i in range(size)])


def dot(a, b):
    return jnp.dot(a, b, preferred_element_type=F32)


def add(a, b):
    return (a.astype(F32) + b.astype(F32)).astype(BF16)


def head_rows(x, rows_ref):
    for h in range(GROUP):
        rows_ref[h * TOK : (h + 1) * TOK, :] = x[:, h * HD : (h + 1) * HD]
    rows_ref[GROUP * TOK :, :] = jnp.zeros((ROWS - GROUP * TOK, HD), rows_ref.dtype)


def flip(x):
    return x.astype(F32).T


def each_tile(step):
    def pair(n, carry):
        for half in range(2):
            step(pl.ds(pl.multiple_of((2 * n + half) * TILE, TILE), TILE))
        return carry

    lax.fori_loop(0, ROWS // (2 * TILE), pair, 0)


def visible_tile(pos, qinfo_ref, cols, chunk):
    query_pos = qinfo_ref[0:1, cols]
    first = jnp.where(chunk < PROMPT // CHUNK, 0, qinfo_ref[1:2, cols])
    return (pos <= query_pos) & (pos >= first)


def chunk_rows(mine_ref, other_ref, first):
    parts = [ref[xh * PART + first : xh * PART + first + TOK, :] for ref in (mine_ref, other_ref) for xh in (0, 1)]
    return jnp.concatenate(parts, 0)


def by_flag(flags_ref, k, step):
    @pl.when(flags_ref[k] == 1)
    def _():
        step(False)

    @pl.when(flags_ref[k] == 2)
    def _():
        step(True)


def prepare_kernel(q_ref, rows_ref, q_t_ref):
    head_rows(q_ref, rows_ref)
    q_t_ref[...] = flip(rows_ref[...]).astype(BF16)


def forward_kernel(ks, flags_ref, chunk_ref, q_t_ref, posr_ref, qinfo_ref, *refs):
    blocks, refs = refs[: 2 * len(ks)], refs[2 * len(ks) :]
    top_ref, sum_ref, acc_ref = refs[-3:]
    if ks[0] == 0:
        top_ref[...] = jnp.full_like(top_ref, NEG)
        sum_ref[...] = jnp.zeros_like(sum_ref)
        acc_ref[...] = jnp.zeros_like(acc_ref)
    else:
        for old, new in zip(refs[:3], refs[3:]):
            new[...] = old[...]

    def step(k, mine_ref, other_ref, masked):
        chunk = chunk_ref[k]
        keys = chunk_rows(mine_ref, other_ref, 0)
        values_t = flip(chunk_rows(mine_ref, other_ref, TOK)).astype(BF16)
        pos = posr_ref[:, 0:1] + chunk * CHUNK

        @each_tile
        def _(cols):
            scores = dot(keys, q_t_ref[:, cols]) * SCALE2
            if masked:
                scores = jnp.where(visible_tile(pos, qinfo_ref, cols, chunk), scores, NEG)
            old = top_ref[0:1, cols]
            top = jnp.maximum(old, jnp.max(scores, axis=0, keepdims=True))
            weights = jnp.exp2(scores - top)
            factor = jnp.exp2(old - top)
            top_ref[0:1, cols] = top
            sum_ref[0:1, cols] = sum_ref[0:1, cols] * factor + jnp.sum(weights, axis=0, keepdims=True)
            acc_ref[:, cols] = acc_ref[:, cols] * factor + dot(values_t, weights.astype(BF16))

    for n, k in enumerate(ks):
        by_flag(flags_ref, k, functools.partial(step, k, blocks[2 * n], blocks[2 * n + 1]))


def project_kernel(chunk_ref, core_ref, top_ref, sum_ref, acc_ref, gy_ref, *refs):
    blocks, refs = refs[: 2 * NZ], refs[2 * NZ :]
    y_ref, g_rows_ref, g_t_ref, delta_ref, lse_ref, attn_ref, weight_ref, grad_ref = refs
    lse_ref[...] = jnp.broadcast_to(top_ref[0:1, :] + jnp.log2(sum_ref[0:1, :]), lse_ref.shape)
    attn_t = (acc_ref[...] / sum_ref[0:1, :]).astype(BF16).astype(F32)
    attn = attn_t.T.astype(BF16)
    for h in range(GROUP):
        attn_ref[:, h * HD : (h + 1) * HD] = attn[h * TOK : (h + 1) * TOK, :]
    core = core_ref[0]
    for k in range(NZ):
        chunk = chunk_ref[k]
        for ref, c in ((blocks[2 * k], core), (blocks[2 * k + 1], 1 - core)):
            for xh in range(2):
                at = pl.ds(pl.multiple_of(xh * 2 * COLS + c * COLS, 32), COLS)
                for h in range(GROUP):
                    first = xh * PART + 2 * TOK + h * COLS
                    weight_ref[at, h * HD : (h + 1) * HD] = ref[first : first + COLS, :]
        weight = weight_ref[...]
        terms = lax.dot_general(attn_ref[...], weight, (((1,), (1,)), ((), ())), preferred_element_type=F32)
        y_ref[pl.ds(pl.multiple_of(chunk * TOK, TOK), TOK), :] = terms.astype(BF16)
        grad = dot(gy_ref[pl.ds(pl.multiple_of(chunk * TOK, TOK), TOK), :], weight)
        grad_ref[...] = grad if k == 0 else grad_ref[...] + grad
    head_rows(grad_ref[...].astype(BF16), g_rows_ref)
    g_t = flip(g_rows_ref[...])
    g_t_ref[...] = g_t.astype(BF16)
    delta_ref[...] = jnp.broadcast_to(jnp.sum(g_t * attn_t, axis=0, keepdims=True), delta_ref.shape)


def backward_kernel(
    ks, flags_ref, chunk_ref, rows_ref, q_t_ref, g_rows_ref, g_t_ref, delta_ref, lse_ref, posr_ref, qinfo_ref, *refs
):
    blocks, refs = refs[: 2 * len(ks)], refs[2 * len(ks) :]
    dk_ref, dv_ref = refs[-2:]
    if ks[0] == NZ // 2:
        outs, dq_ref = refs[: 2 * len(ks)], refs[2 * len(ks)]
        dq_ref[...] = jnp.zeros_like(dq_ref)
    elif ks[0] == 0:
        outs, last_ref, dq_ref = refs[1:3], refs[3], refs[4]
        dq_ref[...] = refs[0][...]
    else:
        outs, dq_ref = refs[1 : 1 + 2 * len(ks)], refs[1 + 2 * len(ks)]
        dq_ref[...] = refs[0][...]

    def step(k, mine_ref, other_ref, dmine_ref, dother_ref, masked):
        chunk = chunk_ref[k]
        keys = chunk_rows(mine_ref, other_ref, 0)
        values = chunk_rows(mine_ref, other_ref, TOK)
        keys_t = flip(keys).astype(BF16)
        dk_ref[...] = jnp.zeros_like(dk_ref)
        dv_ref[...] = jnp.zeros_like(dv_ref)
        pos = posr_ref[:, 0:1] + chunk * CHUNK

        @each_tile
        def _(cols):
            scores = dot(keys, q_t_ref[:, cols]) * SCALE2
            if masked:
                scores = jnp.where(visible_tile(pos, qinfo_ref, cols, chunk), scores, NEG)
            probs = jnp.exp2(scores - lse_ref[0:1, cols])
            dv_ref[...] += dot(probs.astype(BF16), g_rows_ref[cols, :])
            grads = probs * (dot(values, g_t_ref[:, cols]) - delta_ref[0:1, cols])
            grads = grads.astype(BF16)
            dk_ref[...] += dot(grads, rows_ref[cols, :])
            dq_ref[:, cols] += dot(keys_t, grads)
        dk, dv = (dk_ref[...] * SCALE).astype(BF16), dv_ref[...].astype(BF16)
        for n, ref in enumerate((dmine_ref, dmine_ref, dother_ref, dother_ref)):
            at = n % 2 * HALF
            ref[at : at + TOK, :] = dk[n * TOK : (n + 1) * TOK]
            ref[at + TOK : at + HALF, :] = dv[n * TOK : (n + 1) * TOK]

    for n, k in enumerate(ks):
        dmine_ref, dother_ref = outs[2 * n : 2 * n + 2]

        @pl.when(flags_ref[k] == 0)
        def _(dmine_ref=dmine_ref, dother_ref=dother_ref):
            dmine_ref[...] = jnp.zeros_like(dmine_ref)
            dother_ref[...] = jnp.zeros_like(dother_ref)

        by_flag(
            flags_ref, k, functools.partial(step, k, blocks[2 * n], blocks[2 * n + 1], dmine_ref, dother_ref)
        )
    if ks[0] == 0:
        dq = (dq_ref[...].T * SCALE).astype(BF16)
        for h in range(GROUP):
            last_ref[:, h * HD : (h + 1) * HD] = dq[h * TOK : (h + 1) * TOK, :]


SMEM = pl.BlockSpec(memory_space=pltpu.SMEM)
VMEM = pl.BlockSpec(memory_space=pltpu.VMEM)


def call(kernel, name, scalars, arrays, outs, scratch=(), flops=0):
    return pl.pallas_call(
        kernel,
        out_shape=tuple(jax.ShapeDtypeStruct(s, t) for s, t in outs),
        in_specs=[SMEM] * len(scalars) + [VMEM] * len(arrays),
        out_specs=(VMEM,) * len(outs),
        scratch_shapes=[pltpu.VMEM(s, t) for s, t in scratch],
        compiler_params=pltpu.CompilerParams(vmem_limit_bytes=48 << 20),
        cost_estimate=pl.CostEstimate(flops=flops, bytes_accessed=1 << 20, transcendentals=0),
        name=name,
    )(*scalars, *arrays)


def tables(resp_blocks):
    z, xh, c = lax.axis_index("z"), lax.axis_index("xh"), lax.axis_index("c")
    row = jnp.arange(CHUNK, dtype=jnp.int32)
    core = jnp.where(row < HALF, c, 1 - c)
    posr = core * TOK + (row % HALF) // TOK * HALF + row % TOK
    posr = jnp.broadcast_to(posr[:, None], (CHUNK, 128))
    first = z * CHUNK + xh * HALF + c * TOK
    query_pos = first + jnp.arange(ROWS, dtype=jnp.int32) % TOK
    end, start = jnp.int32(PROMPT), jnp.full((ROWS,), PROMPT, jnp.int32)
    for r in range(NRESP - 1):
        end = end + resp_blocks[r] * BLK
        start = jnp.where(query_pos >= end, end, start)
    qinfo = jnp.concatenate([query_pos[None], start[None], jnp.zeros((6, ROWS), jnp.int32)], 0)
    chunks = (z + jnp.arange(NZ, dtype=jnp.int32)) % NZ
    earlier = (chunks < PROMPT // CHUNK) | ((chunks + 1) * CHUNK > jnp.min(start))
    kind = jnp.where(chunks < PROMPT // CHUNK, 1, 2)
    flags = jnp.where(chunks == z, 2, jnp.where((chunks < z) & earlier, kind, 0))
    return flags, chunks, posr, qinfo


STATE = [((8, ROWS), F32), ((8, ROWS), F32), ((HD, ROWS), F32)]


def local(queries, keys, values, w_out, grad_y, resp_blocks):
    xh = lax.axis_index("xh")
    flags, chunks, posr, qinfo = tables(resp_blocks)
    grad_full = lax.all_gather(grad_y, KV, axis=0, tiled=True)
    rows, q_t = call(prepare_kernel, "prepare", (), (queries,), [((ROWS, HD), BF16), ((HD, ROWS), BF16)])

    weight = w_out.reshape(GROUP, HD, COLS).transpose(0, 2, 1).reshape(GROUP * COLS, HD)
    own = jnp.concatenate([keys, values, weight], 0)
    partner = shift(own, "xh", 1, 2)
    own = jnp.where(xh == 0, jnp.concatenate([own, partner], 0), jnp.concatenate([partner, own], 0))
    blocks, state = {}, ()

    def arrive(found, state):
        for k, mine in found:
            blocks[k] = (mine, shift(mine, "c", 1, 2))
        ks = tuple(k for k, _ in found)
        pairs = [b for k in ks for b in blocks[k]]
        return call(
            functools.partial(forward_kernel, ks), "forward", (flags, chunks),
            (q_t, posr, qinfo, *pairs, *state), STATE, flops=len(ks) << 31,
        )

    state = arrive([(0, own)], state)
    up, down = own, own
    for step in range(1, NZ // 2 + 1):
        if step < NZ // 2:
            sent = shift(up, "z", 1, NZ), shift(down, "z", -1, NZ)
        else:
            sent = shift(up[:PART], "z", 1, NZ), shift(down[PART:], "z", -1, NZ)
        if step > 1:
            state = arrive([(NZ + 1 - step, up), (step - 1, down)], state)
        if step == NZ // 2 - 1:
            up, down, state, grad_full = lax.optimization_barrier((*sent, state, grad_full))
        else:
            up, down, state = lax.optimization_barrier((*sent, state))
    state = arrive([(NZ // 2, jnp.concatenate([up, down], 0))], state)

    core = lax.axis_index("c").reshape(1).astype(jnp.int32)
    y_terms, g_rows, g_t, delta, lse = call(
        project_kernel, "project", (chunks, core),
        (*state, grad_full, *[b for k in range(NZ) for b in blocks[k]]),
        [
            ((NKV * TOK, WIDTH), BF16), ((ROWS, HD), BF16), ((HD, ROWS), BF16), ((8, ROWS), F32), ((8, ROWS), F32),
        ],
        [((TOK, WIDTH), BF16), ((4 * COLS, WIDTH), BF16), ((TOK, WIDTH), F32)],
        flops=1 << 32,
    )
    y_out = lax.psum_scatter(y_terms, KV, scatter_dimension=0, tiled=True)

    def leave(ks, dq):
        outs = [((CHUNK, HD), BF16)] * (2 * len(ks))
        outs = outs + [((TOK, WIDTH), BF16)] * (ks[0] == 0) + [((HD, ROWS), F32)]
        pairs = [b for k in ks for b in blocks[k]]
        found = call(
            functools.partial(backward_kernel, ks), "backward", (flags, chunks),
            (rows, q_t, g_rows, g_t, delta, lse, posr, qinfo, *pairs, *dq), outs,
            [((CHUNK, HD), F32)] * 2, flops=len(ks) << 32,
        )
        return found[: 2 * len(ks)], found[2 * len(ks) :]

    def joined(raw):
        return [add(raw[n], shift(raw[n + 1], "c", 1, 2)) for n in range(0, len(raw), 2)]

    raw, dq = leave((NZ // 2,), ())
    (term,) = joined(raw)
    raw, dq = leave((NZ // 2 - 1, NZ // 2 + 1), dq)
    up, down = term[:HALF], term[HALF:]
    for step in range(NZ // 2 - 1, -1, -1):
        up, down, raw, dq = lax.optimization_barrier((up, down, raw, dq))
        sent = shift(up, "z", 1, NZ), shift(down, "z", -1, NZ)
        terms = joined(raw)
        if step > 0:
            raw, dq = leave((step - 1, NZ + 1 - step)[: min(step, 2)], dq)
        (up, down), terms, raw, dq = lax.optimization_barrier((sent, terms, raw, dq))
        if step == 0:
            break
        low, high = terms
        if step == NZ // 2 - 1:
            up = jnp.concatenate([add(low[:HALF], up), low[HALF:]], 0)
            down = jnp.concatenate([high[:HALF], add(high[HALF:], down)], 0)
        else:
            up, down = add(low, up), add(high, down)
    grad_q = dq[0]
    total = terms[0].astype(F32) + (up.astype(F32) + down.astype(F32))
    low, high = total[:HALF], total[HALF:]
    send = jnp.where(xh == 0, high, low).astype(BF16)
    total = jnp.where(xh == 0, low, high) + shift(send, "xh", 1, 2).astype(F32)
    total = total.astype(BF16)
    return y_out, grad_q, total[:TOK], total[TOK:]


def solution(mesh):
    fine = Mesh(mesh.devices.reshape(NZ, 2, 2, 4, 2), CTX + KV)
    both = P(CTX, KV)
    return jax.shard_map(
        local,
        mesh=fine,
        in_specs=(both, both, both, P(KV, CTX), both, P()),
        out_specs=(both,) * 4,
        check_vma=False,
    )
```

```python
import functools
import math

import jax
import jax.numpy as jnp
from jax import lax
from jax.experimental import pallas as pl
from jax.experimental.pallas import tpu as pltpu
from jax.sharding import Mesh
from jax.sharding import PartitionSpec as P

GROUP = 5
HD = 128
BLK = 128
NRESP = 4
NZ = 8
NKV = 8
TOK = 192
COLS = 160
ROWS = 1024
TILE = 256
HALF = 2 * TOK
CHUNK = 4 * TOK
PROMPT = 4 * CHUNK
WPART = GROUP * COLS
WIDTH = GROUP * HD
NEG = -1e30
SCALE = 1.0 / math.sqrt(HD)
SCALE2 = SCALE * math.log2(math.e)
CTX = ("z", "xh", "c")
KV = ("y", "xl")
F32 = jnp.float32
BF16 = jnp.bfloat16


def shift(x, axis, by, size):
    return lax.ppermute(x, axis, [(i, (i + by) % size) for i in range(size)])


def dot(a, b):
    return jnp.dot(a, b, preferred_element_type=F32)


def add(a, b):
    return (a.astype(F32) + b.astype(F32)).astype(BF16)


def head_rows(x, rows_ref):
    for h in range(GROUP):
        rows_ref[h * TOK : (h + 1) * TOK, :] = x[:, h * HD : (h + 1) * HD]
    rows_ref[GROUP * TOK :, :] = jnp.zeros((ROWS - GROUP * TOK, HD), rows_ref.dtype)


def flip(x):
    return x.astype(F32).T


def each_tile(step):
    def pair(n, carry):
        for half in range(2):
            step(pl.ds(pl.multiple_of((2 * n + half) * TILE, TILE), TILE))
        return carry

    lax.fori_loop(0, ROWS // (2 * TILE), pair, 0)


def visible_tile(pos, qinfo_ref, cols, chunk):
    query_pos = qinfo_ref[0:1, cols]
    first = jnp.where(chunk < PROMPT // CHUNK, 0, qinfo_ref[1:2, cols])
    return (pos <= query_pos) & (pos >= first)


def chunk_rows(refs, spots, first):
    return jnp.concatenate([refs[i][at + first : at + first + TOK, :] for i, at in spots], 0)


def by_flag(flags_ref, k, step):
    @pl.when(flags_ref[k] == 1)
    def _():
        step(False)

    @pl.when(flags_ref[k] == 2)
    def _():
        step(True)


def prepare_kernel(q_ref, rows_ref, q_t_ref):
    head_rows(q_ref, rows_ref)
    q_t_ref[...] = flip(rows_ref[...]).astype(BF16)


def forward_kernel(ks, count, spots, flags_ref, chunk_ref, q_t_ref, posr_ref, qinfo_ref, *refs):
    blocks, refs = refs[:count], refs[count:]
    top_ref, sum_ref, acc_ref = refs[-3:]
    if ks[0] == 0:
        top_ref[...] = jnp.full_like(top_ref, NEG)
        sum_ref[...] = jnp.zeros_like(sum_ref)
        acc_ref[...] = jnp.zeros_like(acc_ref)
    else:
        for old, new in zip(refs[:3], refs[3:]):
            new[...] = old[...]

    def step(k, where, masked):
        chunk = chunk_ref[k]
        keys = chunk_rows(blocks, where, 0)
        values_t = flip(chunk_rows(blocks, where, TOK)).astype(BF16)
        pos = posr_ref[:, 0:1] + chunk * CHUNK

        @each_tile
        def _(cols):
            scores = dot(keys, q_t_ref[:, cols]) * SCALE2
            if masked:
                scores = jnp.where(visible_tile(pos, qinfo_ref, cols, chunk), scores, NEG)
            old = top_ref[0:1, cols]
            top = jnp.maximum(old, jnp.max(scores, axis=0, keepdims=True))
            weights = jnp.exp2(scores - top)
            factor = jnp.exp2(old - top)
            top_ref[0:1, cols] = top
            sum_ref[0:1, cols] = sum_ref[0:1, cols] * factor + jnp.sum(weights, axis=0, keepdims=True)
            acc_ref[:, cols] = acc_ref[:, cols] * factor + dot(values_t, weights.astype(BF16))

    for n, k in enumerate(ks):
        by_flag(flags_ref, k, functools.partial(step, k, spots[n]))


def gather_weight(refs, spots, core, weight_ref):
    for own in range(2):

        @pl.when(core == own)
        def _(own=own):
            for n, (i, first) in enumerate(spots):
                at = (n % 2 * 2 + (own if n < 2 else 1 - own)) * COLS
                for h in range(GROUP):
                    rows = refs[i][first + h * COLS : first + (h + 1) * COLS, :]
                    weight_ref[at : at + COLS, h * HD : (h + 1) * HD] = rows


def chunk_at(chunk_ref, k):
    return pl.ds(pl.multiple_of(chunk_ref[k] * TOK, TOK), TOK)


def project_kernel(ks, count, spots, chunk_ref, core_ref, top_ref, sum_ref, acc_ref, gy_ref, *refs):
    blocks, (grad_ref, attn_ref, attn_t_ref, lse_ref, weight_ref) = refs[:count], refs[count:]
    lse_ref[...] = jnp.broadcast_to(top_ref[0:1, :] + jnp.log2(sum_ref[0:1, :]), lse_ref.shape)
    attn_t = acc_ref[...] / sum_ref[0:1, :]
    attn_t_ref[...] = attn_t.astype(BF16)
    attn = attn_t.T.astype(BF16)
    for h in range(GROUP):
        attn_ref[:, h * HD : (h + 1) * HD] = attn[h * TOK : (h + 1) * TOK, :]
    for n, k in enumerate(ks):
        gather_weight(blocks, spots[n], core_ref[0], weight_ref)
        grad = dot(gy_ref[chunk_at(chunk_ref, k), :], weight_ref[...])
        grad_ref[...] = grad if n == 0 else grad_ref[...] + grad


def finish_kernel(ks, count, spots, chunk_ref, core_ref, grad_ref, attn_t_ref, gy_ref, *refs):
    blocks, (g_rows_ref, g_t_ref, delta_ref, weight_ref) = refs[:count], refs[count:]
    gather_weight(blocks, spots[0], core_ref[0], weight_ref)
    grad = grad_ref[...] + dot(gy_ref[chunk_at(chunk_ref, ks[0]), :], weight_ref[...])
    head_rows(grad.astype(BF16), g_rows_ref)
    g_t = flip(g_rows_ref[...])
    g_t_ref[...] = g_t.astype(BF16)
    delta = jnp.sum(g_t * attn_t_ref[...].astype(F32), axis=0, keepdims=True)
    delta_ref[...] = jnp.broadcast_to(delta, delta_ref.shape)


def output_kernel(ks, count, spots, chunk_ref, core_ref, attn_ref, *refs):
    blocks, (y_ref, weight_ref) = refs[:count], refs[count:]
    for n, k in enumerate(ks):
        gather_weight(blocks, spots[n], core_ref[0], weight_ref)
        terms = lax.dot_general(
            attn_ref[...], weight_ref[...], (((1,), (1,)), ((), ())), preferred_element_type=F32
        )
        y_ref[chunk_at(chunk_ref, k), :] = terms.astype(BF16)


def backward_kernel(
    ks, count, spots, flags_ref, chunk_ref, rows_ref, q_t_ref, g_rows_ref, g_t_ref, delta_ref, lse_ref, posr_ref, qinfo_ref, *refs
):
    blocks, refs = refs[:count], refs[count:]
    dk_ref, dv_ref = refs[-2:]
    if ks[0] == NZ // 2:
        old_ref = None
    else:
        old_ref, refs = refs[0], refs[1:]
    outs, others_ref, refs = refs[: len(ks)], refs[len(ks)], refs[len(ks) + 1 :]
    if ks[0] == 0:
        last_ref, refs = refs[0], refs[1:]
    dq_ref = refs[0]
    dq_ref[...] = jnp.zeros_like(dq_ref) if old_ref is None else old_ref[...]

    def step(k, where, dmine_ref, dother_ref, masked):
        chunk = chunk_ref[k]
        keys = chunk_rows(blocks, where, 0)
        values = chunk_rows(blocks, where, TOK)
        keys_t = flip(keys).astype(BF16)
        dk_ref[...] = jnp.zeros_like(dk_ref)
        dv_ref[...] = jnp.zeros_like(dv_ref)
        pos = posr_ref[:, 0:1] + chunk * CHUNK

        @each_tile
        def _(cols):
            scores = dot(keys, q_t_ref[:, cols]) * SCALE2
            if masked:
                scores = jnp.where(visible_tile(pos, qinfo_ref, cols, chunk), scores, NEG)
            probs = jnp.exp2(scores - lse_ref[0:1, cols])
            dv_ref[...] += dot(probs.astype(BF16), g_rows_ref[cols, :])
            grads = probs * (dot(values, g_t_ref[:, cols]) - delta_ref[0:1, cols])
            grads = grads.astype(BF16)
            dk_ref[...] += dot(grads, rows_ref[cols, :])
            dq_ref[:, cols] += dot(keys_t, grads)
        dk, dv = (dk_ref[...] * SCALE).astype(BF16), dv_ref[...].astype(BF16)
        for n, ref in enumerate((dmine_ref, dmine_ref, dother_ref, dother_ref)):
            at = n % 2 * HALF
            ref[at : at + TOK, :] = dk[n * TOK : (n + 1) * TOK]
            ref[at + TOK : at + HALF, :] = dv[n * TOK : (n + 1) * TOK]

    for n, k in enumerate(ks):
        dmine_ref, dother_ref = outs[n], others_ref.at[n * CHUNK : (n + 1) * CHUNK]

        @pl.when(flags_ref[k] == 0)
        def _(dmine_ref=dmine_ref, dother_ref=dother_ref):
            dmine_ref[...] = jnp.zeros_like(dmine_ref)
            dother_ref[...] = jnp.zeros_like(dother_ref)

        by_flag(flags_ref, k, functools.partial(step, k, spots[n], dmine_ref, dother_ref))
    if ks[0] == 0:
        dq = (dq_ref[...].T * SCALE).astype(BF16)
        for h in range(GROUP):
            last_ref[:, h * HD : (h + 1) * HD] = dq[h * TOK : (h + 1) * TOK, :]


SMEM = pl.BlockSpec(memory_space=pltpu.SMEM)
VMEM = pl.BlockSpec(memory_space=pltpu.VMEM)


def call(kernel, name, scalars, arrays, outs, scratch=(), flops=0, mib=20):
    return pl.pallas_call(
        kernel,
        out_shape=tuple(jax.ShapeDtypeStruct(s, t) for s, t in outs),
        in_specs=[SMEM] * len(scalars) + [VMEM] * len(arrays),
        out_specs=(VMEM,) * len(outs),
        scratch_shapes=[pltpu.VMEM(s, t) for s, t in scratch],
        compiler_params=pltpu.CompilerParams(vmem_limit_bytes=mib << 20),
        cost_estimate=pl.CostEstimate(flops=flops, bytes_accessed=1 << 20, transcendentals=0),
        name=name,
    )(*scalars, *arrays)


def tables(resp_blocks):
    z, xh, c = lax.axis_index("z"), lax.axis_index("xh"), lax.axis_index("c")
    row = jnp.arange(CHUNK, dtype=jnp.int32)
    core = jnp.where(row < HALF, c, 1 - c)
    posr = core * TOK + (row % HALF) // TOK * HALF + row % TOK
    posr = jnp.broadcast_to(posr[:, None], (CHUNK, 128))
    first = z * CHUNK + xh * HALF + c * TOK
    query_pos = first + jnp.arange(ROWS, dtype=jnp.int32) % TOK
    end, start = jnp.int32(PROMPT), jnp.full((ROWS,), PROMPT, jnp.int32)
    for r in range(NRESP - 1):
        end = end + resp_blocks[r] * BLK
        start = jnp.where(query_pos >= end, end, start)
    qinfo = jnp.concatenate([query_pos[None], start[None], jnp.zeros((6, ROWS), jnp.int32)], 0)
    chunks = (z + jnp.arange(NZ, dtype=jnp.int32)) % NZ
    earlier = (chunks < PROMPT // CHUNK) | ((chunks + 1) * CHUNK > jnp.min(start))
    kind = jnp.where(chunks < PROMPT // CHUNK, 1, 2)
    flags = jnp.where(chunks == z, 2, jnp.where((chunks < z) & earlier, kind, 0))
    return flags, chunks, posr, qinfo


STATE = [((8, ROWS), F32), ((8, ROWS), F32), ((HD, ROWS), F32)]


def packed(chunks, ks):
    arrays, spots = [], []
    for k in ks:
        found = []
        for array, first in chunks[k]:
            index = next((i for i, known in enumerate(arrays) if known is array), len(arrays))
            if index == len(arrays):
                arrays.append(array)
            found.append((index, first))
        spots.append(tuple(found))
    return arrays, tuple(spots)


def local(queries, keys, values, w_out, grad_y, resp_blocks):
    xh, xl = lax.axis_index("xh"), lax.axis_index("xl")
    core = lax.axis_index("c").reshape(1).astype(jnp.int32)
    far, every = NZ // 2, tuple(range(NZ))
    blocks, weights = {}, {}

    def run(kernel, name, chunks, ks, scalars, arrays, more, outs, scratch=(), mib=20):
        found, spots = packed(chunks, ks)
        body = functools.partial(kernel, ks, len(found), spots)
        return call(body, name, scalars, (*arrays, *found, *more), outs, scratch, flops=1 << 20, mib=mib)

    grad_full = lax.all_gather(grad_y, KV, axis=0, tiled=True)
    kv = jnp.concatenate([keys, values], 0)
    kv_partner = shift(kv, "xh", 1, 2)
    weight = w_out.reshape(GROUP, HD, COLS).transpose(0, 2, 1).reshape(WPART, HD)
    weight_partner = shift(weight, "xh", 1, 2)
    flags, chunks, posr, qinfo = tables(resp_blocks)
    rows, q_t = call(prepare_kernel, "prepare", (), (queries,), [((ROWS, HD), BF16), ((HD, ROWS), BF16)])
    kv_partner, weight, flags, chunks, posr, qinfo, rows, q_t = lax.optimization_barrier(
        (kv_partner, weight, flags, chunks, posr, qinfo, rows, q_t)
    )
    kv = (jnp.where(xh == 0, kv, kv_partner), jnp.where(xh == 0, kv_partner, kv))
    up, down = jnp.concatenate(kv, 0), jnp.concatenate(kv[::-1], 0)
    weight = (jnp.where(xh == 0, weight, weight_partner), jnp.where(xh == 0, weight_partner, weight))
    weight = jnp.concatenate(weight, 0)

    def both_cores(mine, *firsts):
        other = shift(mine, "c", 1, 2)
        return [[(array, first) for array in (mine, other)] for first in firsts]

    def ordered(*pairs):
        return [pair[n] for n in range(2) for pair in pairs]

    def attend(ks, state):
        return run(forward_kernel, "forward", blocks, ks, (flags, chunks), (q_t, posr, qinfo), state, STATE)

    sent = shift(up, "z", 1, NZ), shift(down, "z", -1, NZ)
    blocks[0] = ordered(*both_cores(up, 0, HALF))
    weights[0] = ordered(*both_cores(weight, 0, WPART))
    state = attend((0,), ())
    for step in range(1, far + 1):
        (up, down), state = lax.optimization_barrier((sent, state))
        at = 0 if step == 1 else 2 * WPART
        if step == 1:
            going = jnp.concatenate([weight, up], 0), jnp.concatenate([weight, down], 0)
        elif step == far - 1:
            going = up[: at + HALF], down[: at + HALF]
        elif step == far:
            going = up[:WPART], down[WPART : 2 * WPART]
        else:
            going = up, down
        sent = shift(going[0], "z", 1, NZ), shift(going[1], "z", -1, NZ)
        above, below = both_cores(up, 0, WPART, at, at + HALF), both_cores(down, 0, WPART, at, at + HALF)
        if step > 1:
            weights[NZ + 1 - step], weights[step - 1] = ordered(*above[:2]), ordered(*below[:2])
        if step < far:
            blocks[NZ - step], blocks[step] = ordered(above[2], above[3]), ordered(below[3], below[2])
            state = attend((NZ - step, step), state)
        else:
            blocks[far] = ordered(above[2], below[2])
            state = attend((far,), state)
    near = tuple(k for k in every if k != far)
    grad, attn, attn_t, lse = run(
        project_kernel, "project", weights, near, (chunks, core), (*state, grad_full), (),
        [((TOK, WIDTH), F32), ((TOK, WIDTH), BF16), ((HD, ROWS), BF16), ((8, ROWS), F32)],
        [((4 * COLS, WIDTH), BF16)], mib=32,
    )
    (up, down), grad, attn, attn_t, lse = lax.optimization_barrier((sent, grad, attn, attn_t, lse))
    weights[far] = ordered(both_cores(up, 0)[0], both_cores(down, 0)[0])
    g_rows, g_t, delta = run(
        finish_kernel, "finish", weights, (far,), (chunks, core), (grad, attn_t, grad_full), (),
        [((ROWS, HD), BF16), ((HD, ROWS), BF16), ((8, ROWS), F32)], [((4 * COLS, WIDTH), BF16)],
    )

    def leave(ks, dq):
        outs = [((CHUNK, HD), BF16)] * len(ks) + [((len(ks) * CHUNK, HD), BF16)]
        outs = outs + [((TOK, WIDTH), BF16)] * (ks[0] == 0) + [((HD, ROWS), F32)]
        found = run(
            backward_kernel, "backward", blocks, ks, (flags, chunks),
            (rows, q_t, g_rows, g_t, delta, lse, posr, qinfo), dq, outs, [((CHUNK, HD), F32)] * 2,
        )
        return found[: len(ks) + 1], found[len(ks) + 1 :]

    def joined(raw):
        others = shift(raw[-1], "c", 1, 2)
        return [add(mine, others[n * CHUNK : (n + 1) * CHUNK]) for n, mine in enumerate(raw[:-1])]

    raw, dq = leave((far,), ())
    (term,) = joined(raw)
    raw, dq = leave((far - 1, far + 1), dq)
    up, down, y_terms = term[:HALF], term[HALF:], attn
    for step in range(far - 1, -1, -1):
        if step < far - 1:
            y_terms = ()
        up, down, raw, dq, y_terms = lax.optimization_barrier((up, down, raw, dq, y_terms))
        sent = shift(up, "z", 1, NZ), shift(down, "z", -1, NZ)
        if step == far - 1:
            (y_terms,) = run(
                output_kernel, "output", weights, every, (chunks, core), (y_terms,), (),
                [((NKV * TOK, WIDTH), BF16)], [((4 * COLS, WIDTH), BF16)], mib=32,
            )
        terms = joined(raw)
        if step > 0:
            raw, dq = leave((step - 1, NZ + 1 - step)[: min(step, 2)], dq)
        if step == far - 1:
            y_pair = lax.psum_scatter(y_terms, "y", scatter_dimension=0, tiled=True)
        (up, down), terms, raw, dq, y_terms = lax.optimization_barrier((sent, terms, raw, dq, y_terms))
        if step == 0:
            break
        low, high = terms
        if step == far - 1:
            up = jnp.concatenate([add(low[:HALF], up), low[HALF:]], 0)
            down = jnp.concatenate([high[:HALF], add(high[HALF:], down)], 0)
        else:
            up, down = add(low, up), add(high, down)
    grad_q = dq[0]
    total = terms[0].astype(F32) + (up.astype(F32) + down.astype(F32))
    low, high = total[:HALF], total[HALF:]
    send = jnp.where(xh == 0, high, low).astype(BF16)
    total = jnp.where(xh == 0, low, high) + shift(send, "xh", 1, 2).astype(F32)
    total = total.astype(BF16)
    low, high = y_pair[:TOK], y_pair[TOK:]
    y_partner = shift(jnp.where(xl == 0, high, low), "xl", 1, 2)
    y_out = add(jnp.where(xl == 0, low, high), y_partner)
    return y_out, grad_q, total[:TOK], total[TOK:]


def solution(mesh):
    fine = Mesh(mesh.devices.reshape(NZ, 2, 2, 4, 2), CTX + KV)
    both = P(CTX, KV)
    return jax.shard_map(
        local,
        mesh=fine,
        in_specs=(both, both, both, P(KV, CTX), both, P()),
        out_specs=(both,) * 4,
        check_vma=False,
    )
```

```python
import functools
import math

import jax
import jax.numpy as jnp
from jax import lax
from jax.experimental import pallas as pl
from jax.experimental.pallas import tpu as pltpu
from jax.sharding import Mesh
from jax.sharding import PartitionSpec as P

GROUP = 5
HD = 128
BLK = 128
NRESP = 4
NZ = 8
NKV = 8
TOK = 192
COLS = 160
ROWS = 1024
TILE = 256
HALF = 2 * TOK
CHUNK = 4 * TOK
PROMPT = 4 * CHUNK
WPART = GROUP * COLS
WIDTH = GROUP * HD
NEG = -1e30
SCALE = 1.0 / math.sqrt(HD)
SCALE2 = SCALE * math.log2(math.e)
CTX = ("z", "xh", "c")
KV = ("y", "xl")
F32 = jnp.float32
BF16 = jnp.bfloat16


def shift(x, axis, by, size):
    return lax.ppermute(x, axis, [(i, (i + by) % size) for i in range(size)])


def dot(a, b):
    return jnp.dot(a, b, preferred_element_type=F32)


def add(a, b):
    return (a.astype(F32) + b.astype(F32)).astype(BF16)


def head_rows(x, rows_ref):
    for h in range(GROUP):
        rows_ref[h * TOK : (h + 1) * TOK, :] = x[:, h * HD : (h + 1) * HD]
    rows_ref[GROUP * TOK :, :] = jnp.zeros((ROWS - GROUP * TOK, HD), rows_ref.dtype)


def flip(x):
    return x.astype(F32).T


def each_tile(step):
    def pair(n, carry):
        for half in range(2):
            step(pl.ds(pl.multiple_of((2 * n + half) * TILE, TILE), TILE))
        return carry

    lax.fori_loop(0, ROWS // (2 * TILE), pair, 0)


def visible_tile(pos, qinfo_ref, cols, chunk):
    query_pos = qinfo_ref[0:1, cols]
    first = jnp.where(chunk < PROMPT // CHUNK, 0, qinfo_ref[1:2, cols])
    return (pos <= query_pos) & (pos >= first)


def chunk_rows(refs, spots, first):
    return jnp.concatenate([refs[i][at + first : at + first + TOK, :] for i, at in spots], 0)


def by_flag(flags_ref, k, step):
    @pl.when(flags_ref[k] == 1)
    def _():
        step(False)

    @pl.when(flags_ref[k] == 2)
    def _():
        step(True)


def prepare_kernel(q_ref, rows_ref, q_t_ref):
    head_rows(q_ref, rows_ref)
    q_t_ref[...] = flip(rows_ref[...]).astype(BF16)


def forward_kernel(ks, count, spots, flags_ref, chunk_ref, q_t_ref, posr_ref, qinfo_ref, *refs):
    blocks, refs = refs[:count], refs[count:]
    top_ref, sum_ref, acc_ref = refs[-3:]
    if ks[0] == 0:
        top_ref[...] = jnp.full_like(top_ref, NEG)
        sum_ref[...] = jnp.zeros_like(sum_ref)
        acc_ref[...] = jnp.zeros_like(acc_ref)
    else:
        for old, new in zip(refs[:3], refs[3:]):
            new[...] = old[...]

    def step(k, where, masked):
        chunk = chunk_ref[k]
        keys = chunk_rows(blocks, where, 0)
        values_t = flip(chunk_rows(blocks, where, TOK)).astype(BF16)
        pos = posr_ref[:, 0:1] + chunk * CHUNK

        @each_tile
        def _(cols):
            scores = dot(keys, q_t_ref[:, cols]) * SCALE2
            if masked:
                scores = jnp.where(visible_tile(pos, qinfo_ref, cols, chunk), scores, NEG)
            old = top_ref[0:1, cols]
            top = jnp.maximum(old, jnp.max(scores, axis=0, keepdims=True))
            weights = jnp.exp2(scores - top)
            factor = jnp.exp2(old - top)
            top_ref[0:1, cols] = top
            sum_ref[0:1, cols] = sum_ref[0:1, cols] * factor + jnp.sum(weights, axis=0, keepdims=True)
            acc_ref[:, cols] = acc_ref[:, cols] * factor + dot(values_t, weights.astype(BF16))

    for n, k in enumerate(ks):
        by_flag(flags_ref, k, functools.partial(step, k, spots[n]))


def fetch(refs, spots, stage_ref, sem_ref):
    copies = []
    for n, pieces in enumerate(spots):
        for m, (i, first) in enumerate(pieces):
            at = 4 * n + m
            copies.append(
                pltpu.make_async_copy(refs[i].at[first : first + WPART], stage_ref.at[at], sem_ref.at[at])
            )
    for copy in copies:
        copy.start()
    return copies


def gather_weight(copies, n, stage_ref, core, weight_ref):
    for copy in copies[4 * n : 4 * n + 4]:
        copy.wait()
    for own in range(2):

        @pl.when(core == own)
        def _(own=own):
            for m in range(4):
                at = (m % 2 * 2 + (own if m < 2 else 1 - own)) * COLS
                for h in range(GROUP):
                    rows = stage_ref[4 * n + m, h * COLS : (h + 1) * COLS, :]
                    weight_ref[at : at + COLS, h * HD : (h + 1) * HD] = rows


def chunk_at(chunk_ref, k):
    return pl.ds(pl.multiple_of(chunk_ref[k] * TOK, TOK), TOK)


def project_kernel(ks, count, spots, chunk_ref, core_ref, top_ref, sum_ref, acc_ref, gy_ref, *refs):
    blocks, refs = refs[:count], refs[count:]
    grad_ref, attn_ref, attn_t_ref, lse_ref, weight_ref, stage_ref, here_ref, sem_ref = refs
    bring = pltpu.make_async_copy(gy_ref, here_ref, sem_ref.at[4 * len(ks)])
    bring.start()
    copies = fetch(blocks, spots, stage_ref, sem_ref)
    lse_ref[...] = jnp.broadcast_to(top_ref[0:1, :] + jnp.log2(sum_ref[0:1, :]), lse_ref.shape)
    attn_t = acc_ref[...] / sum_ref[0:1, :]
    attn_t_ref[...] = attn_t.astype(BF16)
    attn = attn_t.T.astype(BF16)
    for h in range(GROUP):
        attn_ref[:, h * HD : (h + 1) * HD] = attn[h * TOK : (h + 1) * TOK, :]
    bring.wait()
    for n, k in enumerate(ks):
        gather_weight(copies, n, stage_ref, core_ref[0], weight_ref)
        grad = dot(here_ref[chunk_at(chunk_ref, k), :], weight_ref[...])
        grad_ref[...] = grad if n == 0 else grad_ref[...] + grad


def finish_kernel(ks, count, spots, chunk_ref, core_ref, grad_ref, attn_t_ref, gy_ref, *refs):
    blocks, refs = refs[:count], refs[count:]
    g_rows_ref, g_t_ref, delta_ref, weight_ref, stage_ref, here_ref, sem_ref = refs
    bring = pltpu.make_async_copy(gy_ref.at[chunk_at(chunk_ref, ks[0])], here_ref, sem_ref.at[4])
    bring.start()
    copies = fetch(blocks, spots, stage_ref, sem_ref)
    bring.wait()
    gather_weight(copies, 0, stage_ref, core_ref[0], weight_ref)
    grad = grad_ref[...] + dot(here_ref[...], weight_ref[...])
    head_rows(grad.astype(BF16), g_rows_ref)
    g_t = flip(g_rows_ref[...])
    g_t_ref[...] = g_t.astype(BF16)
    delta = jnp.sum(g_t * attn_t_ref[...].astype(F32), axis=0, keepdims=True)
    delta_ref[...] = jnp.broadcast_to(delta, delta_ref.shape)


def output_kernel(ks, count, spots, chunk_ref, core_ref, attn_ref, *refs):
    blocks, (y_ref, weight_ref, stage_ref, sem_ref) = refs[:count], refs[count:]
    copies = fetch(blocks, spots, stage_ref, sem_ref)
    for n, k in enumerate(ks):
        gather_weight(copies, n, stage_ref, core_ref[0], weight_ref)
        terms = lax.dot_general(
            attn_ref[...], weight_ref[...], (((1,), (1,)), ((), ())), preferred_element_type=F32
        )
        y_ref[chunk_at(chunk_ref, k), :] = terms.astype(BF16)


def backward_kernel(
    ks, count, spots, flags_ref, chunk_ref, rows_ref, q_t_ref, g_rows_ref, g_t_ref, delta_ref, lse_ref, posr_ref, qinfo_ref, *refs
):
    blocks, refs = refs[:count], refs[count:]
    dk_ref, dv_ref = refs[-2:]
    if ks[0] == NZ // 2:
        old_ref = None
    else:
        old_ref, refs = refs[0], refs[1:]
    outs, others_ref, refs = refs[: len(ks)], refs[len(ks)], refs[len(ks) + 1 :]
    if ks[0] == 0:
        last_ref, refs = refs[0], refs[1:]
    dq_ref = refs[0]
    dq_ref[...] = jnp.zeros_like(dq_ref) if old_ref is None else old_ref[...]

    def step(k, where, dmine_ref, dother_ref, masked):
        chunk = chunk_ref[k]
        keys = chunk_rows(blocks, where, 0)
        values = chunk_rows(blocks, where, TOK)
        keys_t = flip(keys).astype(BF16)
        dk_ref[...] = jnp.zeros_like(dk_ref)
        dv_ref[...] = jnp.zeros_like(dv_ref)
        pos = posr_ref[:, 0:1] + chunk * CHUNK

        @each_tile
        def _(cols):
            scores = dot(keys, q_t_ref[:, cols]) * SCALE2
            if masked:
                scores = jnp.where(visible_tile(pos, qinfo_ref, cols, chunk), scores, NEG)
            probs = jnp.exp2(scores - lse_ref[0:1, cols])
            dv_ref[...] += dot(probs.astype(BF16), g_rows_ref[cols, :])
            grads = probs * (dot(values, g_t_ref[:, cols]) - delta_ref[0:1, cols])
            grads = grads.astype(BF16)
            dk_ref[...] += dot(grads, rows_ref[cols, :])
            dq_ref[:, cols] += dot(keys_t, grads)
        dk, dv = (dk_ref[...] * SCALE).astype(BF16), dv_ref[...].astype(BF16)
        for n, ref in enumerate((dmine_ref, dmine_ref, dother_ref, dother_ref)):
            at = n % 2 * HALF
            ref[at : at + TOK, :] = dk[n * TOK : (n + 1) * TOK]
            ref[at + TOK : at + HALF, :] = dv[n * TOK : (n + 1) * TOK]

    for n, k in enumerate(ks):
        dmine_ref, dother_ref = outs[n], others_ref.at[n * CHUNK : (n + 1) * CHUNK]

        @pl.when(flags_ref[k] == 0)
        def _(dmine_ref=dmine_ref, dother_ref=dother_ref):
            dmine_ref[...] = jnp.zeros_like(dmine_ref)
            dother_ref[...] = jnp.zeros_like(dother_ref)

        by_flag(flags_ref, k, functools.partial(step, k, spots[n], dmine_ref, dother_ref))
    if ks[0] == 0:
        dq = (dq_ref[...].T * SCALE).astype(BF16)
        for h in range(GROUP):
            last_ref[:, h * HD : (h + 1) * HD] = dq[h * TOK : (h + 1) * TOK, :]


SMEM = pl.BlockSpec(memory_space=pltpu.SMEM)
VMEM = pl.BlockSpec(memory_space=pltpu.VMEM)


def call(kernel, name, scalars, arrays, outs, scratch=(), loose=(), flops=1 << 20):
    return pl.pallas_call(
        kernel,
        out_shape=tuple(jax.ShapeDtypeStruct(s, t) for s, t in outs),
        in_specs=[SMEM] * len(scalars) + [VMEM] * len(arrays) + [pl.BlockSpec(memory_space=pl.ANY)] * len(loose),
        out_specs=(VMEM,) * len(outs),
        scratch_shapes=[pltpu.VMEM(*s) if isinstance(s, tuple) else s for s in scratch],
        compiler_params=pltpu.CompilerParams(vmem_limit_bytes=58 << 20),
        cost_estimate=pl.CostEstimate(flops=flops, bytes_accessed=1 << 20, transcendentals=0),
        name=name,
    )(*scalars, *arrays, *loose)


def tables(resp_blocks):
    z, xh, c = lax.axis_index("z"), lax.axis_index("xh"), lax.axis_index("c")
    row = jnp.arange(CHUNK, dtype=jnp.int32)
    core = jnp.where(row < HALF, c, 1 - c)
    posr = core * TOK + (row % HALF) // TOK * HALF + row % TOK
    posr = jnp.broadcast_to(posr[:, None], (CHUNK, 128))
    first = z * CHUNK + xh * HALF + c * TOK
    query_pos = first + jnp.arange(ROWS, dtype=jnp.int32) % TOK
    end, start = jnp.int32(PROMPT), jnp.full((ROWS,), PROMPT, jnp.int32)
    for r in range(NRESP - 1):
        end = end + resp_blocks[r] * BLK
        start = jnp.where(query_pos >= end, end, start)
    qinfo = jnp.concatenate([query_pos[None], start[None], jnp.zeros((6, ROWS), jnp.int32)], 0)
    chunks = (z + jnp.arange(NZ, dtype=jnp.int32)) % NZ
    earlier = (chunks < PROMPT // CHUNK) | ((chunks + 1) * CHUNK > jnp.min(start))
    kind = jnp.where(chunks < PROMPT // CHUNK, 1, 2)
    flags = jnp.where(chunks == z, 2, jnp.where((chunks < z) & earlier, kind, 0))
    return flags, chunks, posr, qinfo


STATE = [((8, ROWS), F32), ((8, ROWS), F32), ((HD, ROWS), F32)]


def packed(chunks, ks):
    arrays, spots = [], []
    for k in ks:
        found = []
        for array, first in chunks[k]:
            index = next((i for i, known in enumerate(arrays) if known is array), len(arrays))
            if index == len(arrays):
                arrays.append(array)
            found.append((index, first))
        spots.append(tuple(found))
    return arrays, tuple(spots)


def local(queries, keys, values, w_out, grad_y, resp_blocks):
    xh, xl = lax.axis_index("xh"), lax.axis_index("xl")
    core = lax.axis_index("c").reshape(1).astype(jnp.int32)
    far, every = NZ // 2, tuple(range(NZ))
    blocks, weights = {}, {}

    def run(kernel, name, chunks, ks, scalars, arrays, more, outs, scratch=()):
        found, spots = packed(chunks, ks)
        body = functools.partial(kernel, ks, len(found), spots)
        return call(body, name, scalars, (*arrays, *found, *more), outs, scratch)

    def weigh(kernel, name, ks, arrays, loose, outs, scratch=()):
        found, spots = packed(weights, ks)
        body = functools.partial(kernel, ks, len(found), spots)
        scratch = [
            ((4 * COLS, WIDTH), BF16), ((4 * len(ks), WPART, HD), BF16), *scratch,
            pltpu.SemaphoreType.DMA((4 * len(ks) + 1,)),
        ]
        return call(body, name, (chunks, core), arrays, outs, scratch, (*loose, *found))

    grad_full = lax.all_gather(grad_y, KV, axis=0, tiled=True)
    kv = jnp.concatenate([keys, values], 0)
    kv_partner = shift(kv, "xh", 1, 2)
    weight = w_out.reshape(GROUP, HD, COLS).transpose(0, 2, 1).reshape(WPART, HD)
    weight_partner = shift(weight, "xh", 1, 2)
    flags, chunks, posr, qinfo = tables(resp_blocks)
    rows, q_t = call(prepare_kernel, "prepare", (), (queries,), [((ROWS, HD), BF16), ((HD, ROWS), BF16)])
    kv_partner, weight, flags, chunks, posr, qinfo, rows, q_t = lax.optimization_barrier(
        (kv_partner, weight, flags, chunks, posr, qinfo, rows, q_t)
    )
    kv = (jnp.where(xh == 0, kv, kv_partner), jnp.where(xh == 0, kv_partner, kv))
    up, down = jnp.concatenate(kv, 0), jnp.concatenate(kv[::-1], 0)
    weight = (jnp.where(xh == 0, weight, weight_partner), jnp.where(xh == 0, weight_partner, weight))
    weight = jnp.concatenate(weight, 0)

    def both_cores(mine, *firsts):
        other = shift(mine, "c", 1, 2)
        return [[(array, first) for array in (mine, other)] for first in firsts]

    def ordered(*pairs):
        return [pair[n] for n in range(2) for pair in pairs]

    def attend(ks, state):
        return run(forward_kernel, "forward", blocks, ks, (flags, chunks), (q_t, posr, qinfo), state, STATE)

    sent = shift(up, "z", 1, NZ), shift(down, "z", -1, NZ)
    blocks[0] = ordered(*both_cores(up, 0, HALF))
    weights[0] = ordered(*both_cores(weight, 0, WPART))
    state = attend((0,), ())
    for step in range(1, far + 1):
        (up, down), state = lax.optimization_barrier((sent, state))
        at = 0 if step == 1 else 2 * WPART
        if step == 1:
            going = jnp.concatenate([weight, up], 0), jnp.concatenate([weight, down], 0)
        elif step == far - 1:
            going = up[: at + HALF], down[: at + HALF]
        elif step == far:
            going = up[:WPART], down[WPART : 2 * WPART]
        else:
            going = up, down
        sent = shift(going[0], "z", 1, NZ), shift(going[1], "z", -1, NZ)
        above, below = both_cores(up, 0, WPART, at, at + HALF), both_cores(down, 0, WPART, at, at + HALF)
        if step > 1:
            weights[NZ + 1 - step], weights[step - 1] = ordered(*above[:2]), ordered(*below[:2])
        if step < far:
            blocks[NZ - step], blocks[step] = ordered(above[2], above[3]), ordered(below[3], below[2])
            state = attend((NZ - step, step), state)
        else:
            blocks[far] = ordered(above[2], below[2])
            state = attend((far,), state)
    near = tuple(k for k in every if k != far)
    grad, attn, attn_t, lse = weigh(
        project_kernel, "project", near, state, (grad_full,),
        [((TOK, WIDTH), F32), ((TOK, WIDTH), BF16), ((HD, ROWS), BF16), ((8, ROWS), F32)],
        [((NKV * TOK, WIDTH), BF16)],
    )
    (up, down), grad, attn, attn_t, lse = lax.optimization_barrier((sent, grad, attn, attn_t, lse))
    weights[far] = ordered(both_cores(up, 0)[0], both_cores(down, 0)[0])
    g_rows, g_t, delta = weigh(
        finish_kernel, "finish", (far,), (grad, attn_t), (grad_full,),
        [((ROWS, HD), BF16), ((HD, ROWS), BF16), ((8, ROWS), F32)], [((TOK, WIDTH), BF16)],
    )

    def leave(ks, dq):
        outs = [((CHUNK, HD), BF16)] * len(ks) + [((len(ks) * CHUNK, HD), BF16)]
        outs = outs + [((TOK, WIDTH), BF16)] * (ks[0] == 0) + [((HD, ROWS), F32)]
        found = run(
            backward_kernel, "backward", blocks, ks, (flags, chunks),
            (rows, q_t, g_rows, g_t, delta, lse, posr, qinfo), dq, outs, [((CHUNK, HD), F32)] * 2,
        )
        return found[: len(ks) + 1], found[len(ks) + 1 :]

    def joined(raw):
        others = shift(raw[-1], "c", 1, 2)
        return [add(mine, others[n * CHUNK : (n + 1) * CHUNK]) for n, mine in enumerate(raw[:-1])]

    raw, dq = leave((far,), ())
    (term,) = joined(raw)
    raw, dq = leave((far - 1, far + 1), dq)
    up, down, y_terms = term[:HALF], term[HALF:], attn
    for step in range(far - 1, -1, -1):
        if step < far - 1:
            y_terms = ()
        up, down, raw, dq, y_terms = lax.optimization_barrier((up, down, raw, dq, y_terms))
        sent = shift(up, "z", 1, NZ), shift(down, "z", -1, NZ)
        if step == far - 1:
            (y_terms,) = weigh(output_kernel, "output", every, (y_terms,), (), [((NKV * TOK, WIDTH), BF16)])
        terms = joined(raw)
        if step > 0:
            raw, dq = leave((step - 1, NZ + 1 - step)[: min(step, 2)], dq)
        if step == far - 1:
            y_terms, terms = lax.optimization_barrier((y_terms, terms))
            y_pair = lax.psum_scatter(y_terms, "y", scatter_dimension=0, tiled=True)
        (up, down), terms, raw, dq, y_terms = lax.optimization_barrier((sent, terms, raw, dq, y_terms))
        if step == 0:
            break
        low, high = terms
        if step == far - 1:
            up = jnp.concatenate([add(low[:HALF], up), low[HALF:]], 0)
            down = jnp.concatenate([high[:HALF], add(high[HALF:], down)], 0)
        else:
            up, down = add(low, up), add(high, down)
    grad_q = dq[0]
    total = terms[0].astype(F32) + (up.astype(F32) + down.astype(F32))
    low, high = total[:HALF], total[HALF:]
    send = jnp.where(xh == 0, high, low).astype(BF16)
    total = jnp.where(xh == 0, low, high) + shift(send, "xh", 1, 2).astype(F32)
    total = total.astype(BF16)
    low, high = y_pair[:TOK], y_pair[TOK:]
    y_partner = shift(jnp.where(xl == 0, high, low), "xl", 1, 2)
    y_out = add(jnp.where(xl == 0, low, high), y_partner)
    return y_out, grad_q, total[:TOK], total[TOK:]


def solution(mesh):
    fine = Mesh(mesh.devices.reshape(NZ, 2, 2, 4, 2), CTX + KV)
    both = P(CTX, KV)
    return jax.shard_map(
        local,
        mesh=fine,
        in_specs=(both, both, both, P(KV, CTX), both, P()),
        out_specs=(both,) * 4,
        check_vma=False,
    )
```

```python
import functools
import math

import jax
import jax.numpy as jnp
from jax import lax
from jax.experimental import pallas as pl
from jax.experimental.pallas import tpu as pltpu
from jax.sharding import Mesh
from jax.sharding import PartitionSpec as P

GROUP = 5
HD = 128
BLK = 128
NRESP = 4
NZ = 8
NKV = 8
TOK = 192
COLS = 160
ROWS = 1024
TILE = 256
HALF = 2 * TOK
CHUNK = 4 * TOK
PROMPT = 4 * CHUNK
PART = 2 * TOK + GROUP * COLS
WIDTH = GROUP * HD
NEG = -1e30
SCALE = 1.0 / math.sqrt(HD)
SCALE2 = SCALE * math.log2(math.e)
CTX = ("z", "xh", "c")
KV = ("y", "xl")
F32 = jnp.float32
BF16 = jnp.bfloat16


def shift(x, axis, by, size):
    return lax.ppermute(x, axis, [(i, (i + by) % size) for i in range(size)])


def dot(a, b):
    return jnp.dot(a, b, preferred_element_type=F32)


def add(a, b):
    return (a.astype(F32) + b.astype(F32)).astype(BF16)


def head_rows(x, rows_ref):
    for h in range(GROUP):
        rows_ref[h * TOK : (h + 1) * TOK, :] = x[:, h * HD : (h + 1) * HD]
    rows_ref[GROUP * TOK :, :] = jnp.zeros((ROWS - GROUP * TOK, HD), rows_ref.dtype)


def flip(x):
    return x.astype(F32).T


def each_tile(step):
    def pair(n, carry):
        for half in range(2):
            step(pl.ds(pl.multiple_of((2 * n + half) * TILE, TILE), TILE))
        return carry

    lax.fori_loop(0, ROWS // (2 * TILE), pair, 0)


def visible_tile(pos, qinfo_ref, cols, chunk):
    query_pos = qinfo_ref[0:1, cols]
    first = jnp.where(chunk < PROMPT // CHUNK, 0, qinfo_ref[1:2, cols])
    return (pos <= query_pos) & (pos >= first)


def chunk_rows(mine_ref, other_ref, first):
    parts = [ref[xh * PART + first : xh * PART + first + TOK, :] for ref in (mine_ref, other_ref) for xh in (0, 1)]
    return jnp.concatenate(parts, 0)


def by_flag(flags_ref, k, step):
    @pl.when(flags_ref[k] == 1)
    def _():
        step(False)

    @pl.when(flags_ref[k] == 2)
    def _():
        step(True)


def prepare_kernel(q_ref, rows_ref, q_t_ref):
    head_rows(q_ref, rows_ref)
    q_t_ref[...] = flip(rows_ref[...]).astype(BF16)


def forward_kernel(ks, flags_ref, chunk_ref, q_t_ref, posr_ref, qinfo_ref, *refs):
    blocks, refs = refs[: 2 * len(ks)], refs[2 * len(ks) :]
    top_ref, sum_ref, acc_ref = refs[-3:]
    if ks[0] == 0:
        top_ref[...] = jnp.full_like(top_ref, NEG)
        sum_ref[...] = jnp.zeros_like(sum_ref)
        acc_ref[...] = jnp.zeros_like(acc_ref)
    else:
        for old, new in zip(refs[:3], refs[3:]):
            new[...] = old[...]

    def step(k, mine_ref, other_ref, masked):
        chunk = chunk_ref[k]
        keys = chunk_rows(mine_ref, other_ref, 0)
        values_t = flip(chunk_rows(mine_ref, other_ref, TOK)).astype(BF16)
        pos = posr_ref[:, 0:1] + chunk * CHUNK

        @each_tile
        def _(cols):
            scores = dot(keys, q_t_ref[:, cols]) * SCALE2
            if masked:
                scores = jnp.where(visible_tile(pos, qinfo_ref, cols, chunk), scores, NEG)
            old = top_ref[0:1, cols]
            top = jnp.maximum(old, jnp.max(scores, axis=0, keepdims=True))
            weights = jnp.exp2(scores - top)
            factor = jnp.exp2(old - top)
            top_ref[0:1, cols] = top
            sum_ref[0:1, cols] = sum_ref[0:1, cols] * factor + jnp.sum(weights, axis=0, keepdims=True)
            acc_ref[:, cols] = acc_ref[:, cols] * factor + dot(values_t, weights.astype(BF16))

    for n, k in enumerate(ks):
        by_flag(flags_ref, k, functools.partial(step, k, blocks[2 * n], blocks[2 * n + 1]))


def gather_weight(mine_ref, other_ref, core, weight_ref):
    for own in range(2):

        @pl.when(core == own)
        def _(own=own):
            for ref, c in ((mine_ref, own), (other_ref, 1 - own)):
                for xh in range(2):
                    at = (xh * 2 + c) * COLS
                    for h in range(GROUP):
                        first = xh * PART + 2 * TOK + h * COLS
                        weight_ref[at : at + COLS, h * HD : (h + 1) * HD] = ref[first : first + COLS, :]


def project_kernel(chunk_ref, core_ref, top_ref, sum_ref, acc_ref, gy_ref, *refs):
    blocks, refs = refs[: 2 * NZ], refs[2 * NZ :]
    y_ref, g_rows_ref, g_t_ref, delta_ref, lse_ref, attn_ref, weight_ref, grad_ref = refs
    lse_ref[...] = jnp.broadcast_to(top_ref[0:1, :] + jnp.log2(sum_ref[0:1, :]), lse_ref.shape)
    attn_t = (acc_ref[...] / sum_ref[0:1, :]).astype(BF16).astype(F32)
    attn = attn_t.T.astype(BF16)
    for h in range(GROUP):
        attn_ref[:, h * HD : (h + 1) * HD] = attn[h * TOK : (h + 1) * TOK, :]
    core = core_ref[0]
    for k in range(NZ):
        chunk = chunk_ref[k]
        gather_weight(blocks[2 * k], blocks[2 * k + 1], core, weight_ref)
        weight = weight_ref[...]
        terms = lax.dot_general(attn_ref[...], weight, (((1,), (1,)), ((), ())), preferred_element_type=F32)
        y_ref[pl.ds(pl.multiple_of(chunk * TOK, TOK), TOK), :] = terms.astype(BF16)
        grad = dot(gy_ref[pl.ds(pl.multiple_of(chunk * TOK, TOK), TOK), :], weight)
        grad_ref[...] = grad if k == 0 else grad_ref[...] + grad
    head_rows(grad_ref[...].astype(BF16), g_rows_ref)
    g_t = flip(g_rows_ref[...])
    g_t_ref[...] = g_t.astype(BF16)
    delta_ref[...] = jnp.broadcast_to(jnp.sum(g_t * attn_t, axis=0, keepdims=True), delta_ref.shape)


def backward_kernel(
    ks, flags_ref, chunk_ref, rows_ref, q_t_ref, g_rows_ref, g_t_ref, delta_ref, lse_ref, posr_ref, qinfo_ref, *refs
):
    blocks, refs = refs[: 2 * len(ks)], refs[2 * len(ks) :]
    dk_ref, dv_ref = refs[-2:]
    if ks[0] == NZ // 2:
        old_ref = None
    else:
        old_ref, refs = refs[0], refs[1:]
    outs, others_ref, refs = refs[: len(ks)], refs[len(ks)], refs[len(ks) + 1 :]
    if ks[0] == 0:
        last_ref, refs = refs[0], refs[1:]
    dq_ref = refs[0]
    dq_ref[...] = jnp.zeros_like(dq_ref) if old_ref is None else old_ref[...]

    def step(k, mine_ref, other_ref, dmine_ref, dother_ref, masked):
        chunk = chunk_ref[k]
        keys = chunk_rows(mine_ref, other_ref, 0)
        values = chunk_rows(mine_ref, other_ref, TOK)
        keys_t = flip(keys).astype(BF16)
        dk_ref[...] = jnp.zeros_like(dk_ref)
        dv_ref[...] = jnp.zeros_like(dv_ref)
        pos = posr_ref[:, 0:1] + chunk * CHUNK

        @each_tile
        def _(cols):
            scores = dot(keys, q_t_ref[:, cols]) * SCALE2
            if masked:
                scores = jnp.where(visible_tile(pos, qinfo_ref, cols, chunk), scores, NEG)
            probs = jnp.exp2(scores - lse_ref[0:1, cols])
            dv_ref[...] += dot(probs.astype(BF16), g_rows_ref[cols, :])
            grads = probs * (dot(values, g_t_ref[:, cols]) - delta_ref[0:1, cols])
            grads = grads.astype(BF16)
            dk_ref[...] += dot(grads, rows_ref[cols, :])
            dq_ref[:, cols] += dot(keys_t, grads)
        dk, dv = (dk_ref[...] * SCALE).astype(BF16), dv_ref[...].astype(BF16)
        for n, ref in enumerate((dmine_ref, dmine_ref, dother_ref, dother_ref)):
            at = n % 2 * HALF
            ref[at : at + TOK, :] = dk[n * TOK : (n + 1) * TOK]
            ref[at + TOK : at + HALF, :] = dv[n * TOK : (n + 1) * TOK]

    for n, k in enumerate(ks):
        dmine_ref, dother_ref = outs[n], others_ref.at[n * CHUNK : (n + 1) * CHUNK]

        @pl.when(flags_ref[k] == 0)
        def _(dmine_ref=dmine_ref, dother_ref=dother_ref):
            dmine_ref[...] = jnp.zeros_like(dmine_ref)
            dother_ref[...] = jnp.zeros_like(dother_ref)

        by_flag(
            flags_ref, k, functools.partial(step, k, blocks[2 * n], blocks[2 * n + 1], dmine_ref, dother_ref)
        )
    if ks[0] == 0:
        dq = (dq_ref[...].T * SCALE).astype(BF16)
        for h in range(GROUP):
            last_ref[:, h * HD : (h + 1) * HD] = dq[h * TOK : (h + 1) * TOK, :]


SMEM = pl.BlockSpec(memory_space=pltpu.SMEM)
VMEM = pl.BlockSpec(memory_space=pltpu.VMEM)


def call(kernel, name, scalars, arrays, outs, scratch=(), flops=0, mib=48):
    return pl.pallas_call(
        kernel,
        out_shape=tuple(jax.ShapeDtypeStruct(s, t) for s, t in outs),
        in_specs=[SMEM] * len(scalars) + [VMEM] * len(arrays),
        out_specs=(VMEM,) * len(outs),
        scratch_shapes=[pltpu.VMEM(s, t) for s, t in scratch],
        compiler_params=pltpu.CompilerParams(vmem_limit_bytes=mib << 20),
        cost_estimate=pl.CostEstimate(flops=flops, bytes_accessed=1 << 20, transcendentals=0),
        name=name,
    )(*scalars, *arrays)


def tables(resp_blocks):
    z, xh, c = lax.axis_index("z"), lax.axis_index("xh"), lax.axis_index("c")
    row = jnp.arange(CHUNK, dtype=jnp.int32)
    core = jnp.where(row < HALF, c, 1 - c)
    posr = core * TOK + (row % HALF) // TOK * HALF + row % TOK
    posr = jnp.broadcast_to(posr[:, None], (CHUNK, 128))
    first = z * CHUNK + xh * HALF + c * TOK
    query_pos = first + jnp.arange(ROWS, dtype=jnp.int32) % TOK
    end, start = jnp.int32(PROMPT), jnp.full((ROWS,), PROMPT, jnp.int32)
    for r in range(NRESP - 1):
        end = end + resp_blocks[r] * BLK
        start = jnp.where(query_pos >= end, end, start)
    qinfo = jnp.concatenate([query_pos[None], start[None], jnp.zeros((6, ROWS), jnp.int32)], 0)
    chunks = (z + jnp.arange(NZ, dtype=jnp.int32)) % NZ
    earlier = (chunks < PROMPT // CHUNK) | ((chunks + 1) * CHUNK > jnp.min(start))
    kind = jnp.where(chunks < PROMPT // CHUNK, 1, 2)
    flags = jnp.where(chunks == z, 2, jnp.where((chunks < z) & earlier, kind, 0))
    return flags, chunks, posr, qinfo


STATE = [((8, ROWS), F32), ((8, ROWS), F32), ((HD, ROWS), F32)]


def local(queries, keys, values, w_out, grad_y, resp_blocks):
    xh, xl = lax.axis_index("xh"), lax.axis_index("xl")
    flags, chunks, posr, qinfo = tables(resp_blocks)
    grad_full = lax.all_gather(grad_y, KV, axis=0, tiled=True)
    rows, q_t = call(prepare_kernel, "prepare", (), (queries,), [((ROWS, HD), BF16), ((HD, ROWS), BF16)])

    weight = w_out.reshape(GROUP, HD, COLS).transpose(0, 2, 1).reshape(GROUP * COLS, HD)
    own = jnp.concatenate([keys, values, weight], 0)
    partner = shift(own, "xh", 1, 2)
    partner, flags, chunks, posr, qinfo, rows, q_t = lax.optimization_barrier(
        (partner, flags, chunks, posr, qinfo, rows, q_t)
    )
    own = jnp.where(xh == 0, jnp.concatenate([own, partner], 0), jnp.concatenate([partner, own], 0))
    blocks, state = {}, ()

    def arrive(found, state):
        for k, mine in found:
            blocks[k] = (mine, shift(mine, "c", 1, 2))
        ks = tuple(k for k, _ in found)
        pairs = [b for k in ks for b in blocks[k]]
        return call(
            functools.partial(forward_kernel, ks), "forward", (flags, chunks),
            (q_t, posr, qinfo, *pairs, *state), STATE, flops=len(ks) << 31,
        )

    state = arrive([(0, own)], state)
    up, down = own, own
    for step in range(1, NZ // 2 + 1):
        if step < NZ // 2:
            sent = shift(up, "z", 1, NZ), shift(down, "z", -1, NZ)
        else:
            sent = shift(up[:PART], "z", 1, NZ), shift(down[PART:], "z", -1, NZ)
        if step > 1:
            state = arrive([(NZ + 1 - step, up), (step - 1, down)], state)
        if step == NZ // 2 - 1:
            up, down, state, grad_full = lax.optimization_barrier((*sent, state, grad_full))
        else:
            up, down, state = lax.optimization_barrier((*sent, state))
    state = arrive([(NZ // 2, jnp.concatenate([up, down], 0))], state)

    core = lax.axis_index("c").reshape(1).astype(jnp.int32)
    y_terms, g_rows, g_t, delta, lse = call(
        project_kernel, "project", (chunks, core),
        (*state, grad_full, *[b for k in range(NZ) for b in blocks[k]]),
        [
            ((NKV * TOK, WIDTH), BF16), ((ROWS, HD), BF16), ((HD, ROWS), BF16), ((8, ROWS), F32), ((8, ROWS), F32),
        ],
        [((TOK, WIDTH), BF16), ((4 * COLS, WIDTH), BF16), ((TOK, WIDTH), F32)],
        flops=1 << 32, mib=48,
    )
    y_pair = lax.psum_scatter(y_terms, "y", scatter_dimension=0, tiled=True)

    def leave(ks, dq):
        outs = [((CHUNK, HD), BF16)] * len(ks) + [((len(ks) * CHUNK, HD), BF16)]
        outs = outs + [((TOK, WIDTH), BF16)] * (ks[0] == 0) + [((HD, ROWS), F32)]
        pairs = [b for k in ks for b in blocks[k]]
        found = call(
            functools.partial(backward_kernel, ks), "backward", (flags, chunks),
            (rows, q_t, g_rows, g_t, delta, lse, posr, qinfo, *pairs, *dq), outs,
            [((CHUNK, HD), F32)] * 2, flops=len(ks) << 32,
        )
        return found[: len(ks) + 1], found[len(ks) + 1 :]

    def joined(raw):
        others = shift(raw[-1], "c", 1, 2)
        return [add(mine, others[n * CHUNK : (n + 1) * CHUNK]) for n, mine in enumerate(raw[:-1])]

    raw, dq = leave((NZ // 2,), ())
    (term,) = joined(raw)
    raw, dq = leave((NZ // 2 - 1, NZ // 2 + 1), dq)
    up, down = term[:HALF], term[HALF:]
    for step in range(NZ // 2 - 1, -1, -1):
        up, down, raw, dq = lax.optimization_barrier((up, down, raw, dq))
        sent = shift(up, "z", 1, NZ), shift(down, "z", -1, NZ)
        terms = joined(raw)
        if step > 0:
            raw, dq = leave((step - 1, NZ + 1 - step)[: min(step, 2)], dq)
        (up, down), terms, raw, dq = lax.optimization_barrier((sent, terms, raw, dq))
        if step == 0:
            break
        low, high = terms
        if step == NZ // 2 - 1:
            up = jnp.concatenate([add(low[:HALF], up), low[HALF:]], 0)
            down = jnp.concatenate([high[:HALF], add(high[HALF:], down)], 0)
        else:
            up, down = add(low, up), add(high, down)
    grad_q = dq[0]
    total = terms[0].astype(F32) + (up.astype(F32) + down.astype(F32))
    low, high = total[:HALF], total[HALF:]
    send = jnp.where(xh == 0, high, low).astype(BF16)
    total = jnp.where(xh == 0, low, high) + shift(send, "xh", 1, 2).astype(F32)
    total = total.astype(BF16)
    low, high = y_pair[:TOK], y_pair[TOK:]
    y_partner = shift(jnp.where(xl == 0, high, low), "xl", 1, 2)
    y_out = add(jnp.where(xl == 0, low, high), y_partner)
    return y_out, grad_q, total[:TOK], total[TOK:]


def solution(mesh):
    fine = Mesh(mesh.devices.reshape(NZ, 2, 2, 4, 2), CTX + KV)
    both = P(CTX, KV)
    return jax.shard_map(
        local,
        mesh=fine,
        in_specs=(both, both, both, P(KV, CTX), both, P()),
        out_specs=(both,) * 4,
        check_vma=False,
    )
```

```python
import functools
import math

import jax
import jax.numpy as jnp
from jax import lax
from jax.experimental import pallas as pl
from jax.experimental.pallas import tpu as pltpu
from jax.sharding import Mesh
from jax.sharding import PartitionSpec as P

GROUP = 5
HD = 128
BLK = 128
NRESP = 4
NZ = 8
NKV = 8
TOK = 192
COLS = 160
ROWS = 1024
TILE = 256
HALF = 2 * TOK
CHUNK = 4 * TOK
PROMPT = 4 * CHUNK
PART = 2 * TOK + GROUP * COLS
WIDTH = GROUP * HD
NEG = -1e30
SCALE = 1.0 / math.sqrt(HD)
SCALE2 = SCALE * math.log2(math.e)
CTX = ("z", "xh", "c")
KV = ("y", "xl")
F32 = jnp.float32
BF16 = jnp.bfloat16


def shift(x, axis, by, size):
    return lax.ppermute(x, axis, [(i, (i + by) % size) for i in range(size)])


def dot(a, b):
    return jnp.dot(a, b, preferred_element_type=F32)


def add(a, b):
    return (a.astype(F32) + b.astype(F32)).astype(BF16)


def head_rows(x, rows_ref):
    for h in range(GROUP):
        rows_ref[h * TOK : (h + 1) * TOK, :] = x[:, h * HD : (h + 1) * HD]
    rows_ref[GROUP * TOK :, :] = jnp.zeros((ROWS - GROUP * TOK, HD), rows_ref.dtype)


def flip(x):
    return x.astype(F32).T


def each_tile(step):
    def pair(n, carry):
        for half in range(2):
            step(pl.ds(pl.multiple_of((2 * n + half) * TILE, TILE), TILE))
        return carry

    lax.fori_loop(0, ROWS // (2 * TILE), pair, 0)


def visible_tile(pos, qinfo_ref, cols, chunk):
    query_pos = qinfo_ref[0:1, cols]
    first = jnp.where(chunk < PROMPT // CHUNK, 0, qinfo_ref[1:2, cols])
    return (pos <= query_pos) & (pos >= first)


def chunk_rows(mine_ref, other_ref, first):
    parts = [ref[xh * PART + first : xh * PART + first + TOK, :] for ref in (mine_ref, other_ref) for xh in (0, 1)]
    return jnp.concatenate(parts, 0)


def by_flag(flags_ref, k, step):
    @pl.when(flags_ref[k] == 1)
    def _():
        step(False)

    @pl.when(flags_ref[k] == 2)
    def _():
        step(True)


def prepare_kernel(q_ref, rows_ref, q_t_ref):
    head_rows(q_ref, rows_ref)
    q_t_ref[...] = flip(rows_ref[...]).astype(BF16)


def forward_kernel(ks, flags_ref, chunk_ref, q_t_ref, posr_ref, qinfo_ref, *refs):
    blocks, refs = refs[: 2 * len(ks)], refs[2 * len(ks) :]
    top_ref, sum_ref, acc_ref = refs[-3:]
    if ks[0] == 0:
        top_ref[...] = jnp.full_like(top_ref, NEG)
        sum_ref[...] = jnp.zeros_like(sum_ref)
        acc_ref[...] = jnp.zeros_like(acc_ref)
    else:
        for old, new in zip(refs[:3], refs[3:]):
            new[...] = old[...]

    def step(k, mine_ref, other_ref, masked):
        chunk = chunk_ref[k]
        keys = chunk_rows(mine_ref, other_ref, 0)
        values_t = flip(chunk_rows(mine_ref, other_ref, TOK)).astype(BF16)
        pos = posr_ref[:, 0:1] + chunk * CHUNK

        @each_tile
        def _(cols):
            scores = dot(keys, q_t_ref[:, cols]) * SCALE2
            if masked:
                scores = jnp.where(visible_tile(pos, qinfo_ref, cols, chunk), scores, NEG)
            old = top_ref[0:1, cols]
            top = jnp.maximum(old, jnp.max(scores, axis=0, keepdims=True))
            weights = jnp.exp2(scores - top)
            factor = jnp.exp2(old - top)
            top_ref[0:1, cols] = top
            sum_ref[0:1, cols] = sum_ref[0:1, cols] * factor + jnp.sum(weights, axis=0, keepdims=True)
            acc_ref[:, cols] = acc_ref[:, cols] * factor + dot(values_t, weights.astype(BF16))

    for n, k in enumerate(ks):
        by_flag(flags_ref, k, functools.partial(step, k, blocks[2 * n], blocks[2 * n + 1]))


def gather_weight(mine_ref, other_ref, core, weight_ref):
    for own in range(2):

        @pl.when(core == own)
        def _(own=own):
            for ref, c in ((mine_ref, own), (other_ref, 1 - own)):
                for xh in range(2):
                    at = (xh * 2 + c) * COLS
                    for h in range(GROUP):
                        first = xh * PART + 2 * TOK + h * COLS
                        weight_ref[at : at + COLS, h * HD : (h + 1) * HD] = ref[first : first + COLS, :]


def project_kernel(chunk_ref, core_ref, top_ref, sum_ref, acc_ref, gy_ref, *refs):
    blocks, refs = refs[: 2 * NZ], refs[2 * NZ :]
    y_ref, g_rows_ref, g_t_ref, delta_ref, lse_ref, attn_ref, weight_ref, grad_ref = refs
    lse_ref[...] = jnp.broadcast_to(top_ref[0:1, :] + jnp.log2(sum_ref[0:1, :]), lse_ref.shape)
    attn_t = (acc_ref[...] / sum_ref[0:1, :]).astype(BF16).astype(F32)
    attn = attn_t.T.astype(BF16)
    for h in range(GROUP):
        attn_ref[:, h * HD : (h + 1) * HD] = attn[h * TOK : (h + 1) * TOK, :]
    core = core_ref[0]
    for k in range(NZ):
        chunk = chunk_ref[k]
        gather_weight(blocks[2 * k], blocks[2 * k + 1], core, weight_ref)
        weight = weight_ref[...]
        terms = lax.dot_general(attn_ref[...], weight, (((1,), (1,)), ((), ())), preferred_element_type=F32)
        y_ref[pl.ds(pl.multiple_of(chunk * TOK, TOK), TOK), :] = terms.astype(BF16)
        grad = dot(gy_ref[pl.ds(pl.multiple_of(chunk * TOK, TOK), TOK), :], weight)
        grad_ref[...] = grad if k == 0 else grad_ref[...] + grad
    head_rows(grad_ref[...].astype(BF16), g_rows_ref)
    g_t = flip(g_rows_ref[...])
    g_t_ref[...] = g_t.astype(BF16)
    delta_ref[...] = jnp.broadcast_to(jnp.sum(g_t * attn_t, axis=0, keepdims=True), delta_ref.shape)


def backward_kernel(
    ks, flags_ref, chunk_ref, rows_ref, q_t_ref, g_rows_ref, g_t_ref, delta_ref, lse_ref, posr_ref, qinfo_ref, *refs
):
    blocks, refs = refs[: 2 * len(ks)], refs[2 * len(ks) :]
    dk_ref, dv_ref = refs[-2:]
    if ks[0] == NZ // 2:
        old_ref = None
    else:
        old_ref, refs = refs[0], refs[1:]
    outs, others_ref, refs = refs[: len(ks)], refs[len(ks)], refs[len(ks) + 1 :]
    if ks[0] == 0:
        last_ref, refs = refs[0], refs[1:]
    dq_ref = refs[0]
    dq_ref[...] = jnp.zeros_like(dq_ref) if old_ref is None else old_ref[...]

    def step(k, mine_ref, other_ref, dmine_ref, dother_ref, masked):
        chunk = chunk_ref[k]
        keys = chunk_rows(mine_ref, other_ref, 0)
        values = chunk_rows(mine_ref, other_ref, TOK)
        keys_t = flip(keys).astype(BF16)
        dk_ref[...] = jnp.zeros_like(dk_ref)
        dv_ref[...] = jnp.zeros_like(dv_ref)
        pos = posr_ref[:, 0:1] + chunk * CHUNK

        @each_tile
        def _(cols):
            scores = dot(keys, q_t_ref[:, cols]) * SCALE2
            if masked:
                scores = jnp.where(visible_tile(pos, qinfo_ref, cols, chunk), scores, NEG)
            probs = jnp.exp2(scores - lse_ref[0:1, cols])
            dv_ref[...] += dot(probs.astype(BF16), g_rows_ref[cols, :])
            grads = probs * (dot(values, g_t_ref[:, cols]) - delta_ref[0:1, cols])
            grads = grads.astype(BF16)
            dk_ref[...] += dot(grads, rows_ref[cols, :])
            dq_ref[:, cols] += dot(keys_t, grads)
        dk, dv = (dk_ref[...] * SCALE).astype(BF16), dv_ref[...].astype(BF16)
        for n, ref in enumerate((dmine_ref, dmine_ref, dother_ref, dother_ref)):
            at = n % 2 * HALF
            ref[at : at + TOK, :] = dk[n * TOK : (n + 1) * TOK]
            ref[at + TOK : at + HALF, :] = dv[n * TOK : (n + 1) * TOK]

    for n, k in enumerate(ks):
        dmine_ref, dother_ref = outs[n], others_ref.at[n * CHUNK : (n + 1) * CHUNK]

        @pl.when(flags_ref[k] == 0)
        def _(dmine_ref=dmine_ref, dother_ref=dother_ref):
            dmine_ref[...] = jnp.zeros_like(dmine_ref)
            dother_ref[...] = jnp.zeros_like(dother_ref)

        by_flag(
            flags_ref, k, functools.partial(step, k, blocks[2 * n], blocks[2 * n + 1], dmine_ref, dother_ref)
        )
    if ks[0] == 0:
        dq = (dq_ref[...].T * SCALE).astype(BF16)
        for h in range(GROUP):
            last_ref[:, h * HD : (h + 1) * HD] = dq[h * TOK : (h + 1) * TOK, :]


SMEM = pl.BlockSpec(memory_space=pltpu.SMEM)
VMEM = pl.BlockSpec(memory_space=pltpu.VMEM)


def call(kernel, name, scalars, arrays, outs, scratch=(), flops=0, mib=48):
    return pl.pallas_call(
        kernel,
        out_shape=tuple(jax.ShapeDtypeStruct(s, t) for s, t in outs),
        in_specs=[SMEM] * len(scalars) + [VMEM] * len(arrays),
        out_specs=(VMEM,) * len(outs),
        scratch_shapes=[pltpu.VMEM(s, t) for s, t in scratch],
        compiler_params=pltpu.CompilerParams(vmem_limit_bytes=mib << 20),
        cost_estimate=pl.CostEstimate(flops=flops, bytes_accessed=1 << 20, transcendentals=0),
        name=name,
    )(*scalars, *arrays)


def tables(resp_blocks):
    z, xh, c = lax.axis_index("z"), lax.axis_index("xh"), lax.axis_index("c")
    row = jnp.arange(CHUNK, dtype=jnp.int32)
    core = jnp.where(row < HALF, c, 1 - c)
    posr = core * TOK + (row % HALF) // TOK * HALF + row % TOK
    posr = jnp.broadcast_to(posr[:, None], (CHUNK, 128))
    first = z * CHUNK + xh * HALF + c * TOK
    query_pos = first + jnp.arange(ROWS, dtype=jnp.int32) % TOK
    end, start = jnp.int32(PROMPT), jnp.full((ROWS,), PROMPT, jnp.int32)
    for r in range(NRESP - 1):
        end = end + resp_blocks[r] * BLK
        start = jnp.where(query_pos >= end, end, start)
    qinfo = jnp.concatenate([query_pos[None], start[None], jnp.zeros((6, ROWS), jnp.int32)], 0)
    chunks = (z + jnp.arange(NZ, dtype=jnp.int32)) % NZ
    earlier = (chunks < PROMPT // CHUNK) | ((chunks + 1) * CHUNK > jnp.min(start))
    kind = jnp.where(chunks < PROMPT // CHUNK, 1, 2)
    flags = jnp.where(chunks == z, 2, jnp.where((chunks < z) & earlier, kind, 0))
    return flags, chunks, posr, qinfo


STATE = [((8, ROWS), F32), ((8, ROWS), F32), ((HD, ROWS), F32)]


def local(queries, keys, values, w_out, grad_y, resp_blocks):
    xh, xl = lax.axis_index("xh"), lax.axis_index("xl")
    flags, chunks, posr, qinfo = tables(resp_blocks)
    grad_full = lax.all_gather(grad_y, KV, axis=0, tiled=True)
    rows, q_t = call(prepare_kernel, "prepare", (), (queries,), [((ROWS, HD), BF16), ((HD, ROWS), BF16)])

    weight = w_out.reshape(GROUP, HD, COLS).transpose(0, 2, 1).reshape(GROUP * COLS, HD)
    own = jnp.concatenate([keys, values, weight], 0)
    partner = shift(own, "xh", 1, 2)
    partner, flags, chunks, posr, qinfo, rows, q_t = lax.optimization_barrier(
        (partner, flags, chunks, posr, qinfo, rows, q_t)
    )
    own = jnp.where(xh == 0, jnp.concatenate([own, partner], 0), jnp.concatenate([partner, own], 0))
    blocks, state = {}, ()

    def arrive(found, state):
        for k, mine in found:
            blocks[k] = (mine, shift(mine, "c", 1, 2))
        ks = tuple(k for k, _ in found)
        pairs = [b for k in ks for b in blocks[k]]
        return call(
            functools.partial(forward_kernel, ks), "forward", (flags, chunks),
            (q_t, posr, qinfo, *pairs, *state), STATE, flops=len(ks) << 31,
        )

    state = arrive([(0, own)], state)
    up, down = own, own
    for step in range(1, NZ // 2 + 1):
        if step < NZ // 2:
            sent = shift(up, "z", 1, NZ), shift(down, "z", -1, NZ)
        else:
            sent = shift(up[:PART], "z", 1, NZ), shift(down[PART:], "z", -1, NZ)
        if step > 1:
            state = arrive([(NZ + 1 - step, up), (step - 1, down)], state)
        if step == NZ // 2 - 1:
            up, down, state, grad_full = lax.optimization_barrier((*sent, state, grad_full))
        else:
            up, down, state = lax.optimization_barrier((*sent, state))
    state = arrive([(NZ // 2, jnp.concatenate([up, down], 0))], state)

    core = lax.axis_index("c").reshape(1).astype(jnp.int32)
    y_terms, g_rows, g_t, delta, lse = call(
        project_kernel, "project", (chunks, core),
        (*state, grad_full, *[b for k in range(NZ) for b in blocks[k]]),
        [
            ((NKV * TOK, WIDTH), BF16), ((ROWS, HD), BF16), ((HD, ROWS), BF16), ((8, ROWS), F32), ((8, ROWS), F32),
        ],
        [((TOK, WIDTH), BF16), ((4 * COLS, WIDTH), BF16), ((TOK, WIDTH), F32)],
        flops=1 << 32, mib=48,
    )
    y_pair = lax.psum_scatter(y_terms, "y", scatter_dimension=0, tiled=True)

    def leave(ks, dq):
        outs = [((CHUNK, HD), BF16)] * len(ks) + [((len(ks) * CHUNK, HD), BF16)]
        outs = outs + [((TOK, WIDTH), BF16)] * (ks[0] == 0) + [((HD, ROWS), F32)]
        pairs = [b for k in ks for b in blocks[k]]
        found = call(
            functools.partial(backward_kernel, ks), "backward", (flags, chunks),
            (rows, q_t, g_rows, g_t, delta, lse, posr, qinfo, *pairs, *dq), outs,
            [((CHUNK, HD), F32)] * 2, flops=len(ks) << 32,
        )
        return found[: len(ks) + 1], found[len(ks) + 1 :]

    def joined(raw):
        others = shift(raw[-1], "c", 1, 2)
        return [add(mine, others[n * CHUNK : (n + 1) * CHUNK]) for n, mine in enumerate(raw[:-1])]

    raw, dq = leave((NZ // 2,), ())
    (term,) = joined(raw)
    raw, dq = leave((NZ // 2 - 1, NZ // 2 + 1), dq)
    up, down = term[:HALF], term[HALF:]
    for step in range(NZ // 2 - 1, -1, -1):
        if step == 0:
            up, down, raw, dq, y_pair = lax.optimization_barrier((up, down, raw, dq, y_pair))
        else:
            up, down, raw, dq = lax.optimization_barrier((up, down, raw, dq))
        sent = shift(up, "z", 1, NZ), shift(down, "z", -1, NZ)
        terms = joined(raw)
        if step > 0:
            raw, dq = leave((step - 1, NZ + 1 - step)[: min(step, 2)], dq)
        if step == 0:
            y_low, y_high = y_pair[:TOK], y_pair[TOK:]
            y_partner = shift(jnp.where(xl == 0, y_high, y_low), "xl", 1, 2)
            y_out = add(jnp.where(xl == 0, y_low, y_high), y_partner)
            (up, down), terms, dq, y_out = lax.optimization_barrier((sent, terms, dq, y_out))
            break
        (up, down), terms, raw, dq = lax.optimization_barrier((sent, terms, raw, dq))
        low, high = terms
        if step == NZ // 2 - 1:
            up = jnp.concatenate([add(low[:HALF], up), low[HALF:]], 0)
            down = jnp.concatenate([high[:HALF], add(high[HALF:], down)], 0)
        else:
            up, down = add(low, up), add(high, down)
    grad_q = dq[0]
    total = terms[0].astype(F32) + (up.astype(F32) + down.astype(F32))
    low, high = total[:HALF], total[HALF:]
    send = jnp.where(xh == 0, high, low).astype(BF16)
    total = jnp.where(xh == 0, low, high) + shift(send, "xh", 1, 2).astype(F32)
    total = total.astype(BF16)
    return y_out, grad_q, total[:TOK], total[TOK:]


def solution(mesh):
    fine = Mesh(mesh.devices.reshape(NZ, 2, 2, 4, 2), CTX + KV)
    both = P(CTX, KV)
    return jax.shard_map(
        local,
        mesh=fine,
        in_specs=(both, both, both, P(KV, CTX), both, P()),
        out_specs=(both,) * 4,
        check_vma=False,
    )
```
